128 devices in a mesh: dp: 8 (over x, core), fsdp: 16 (over y, z).
Axes of the slice: x: 4, y: 4, z: 4, core: 2. Of those that a mesh axis runs over, the one named last changes fastest.
Arguments:
- old_states: float32 [3, 2, 34816, 1792], P(None, None, ('dp', 'fsdp')), may hold values from -1.2 to 1.2, as said below
- old_bounds: int32 [8, 17], replicated, may hold values from 0 to 4096, as said below
- new_bounds: int32 [8, 17], replicated, may hold values from 0 to 4096, as said below
- failed: int32 [16], replicated, may hold values from 0 to 7, as said below
- tokens: bfloat16 [4096, 4096], P('fsdp'), may hold values from -6 to 6
- cotangent: bfloat16 [4096, 14336], P('fsdp', 'dp'), may hold values from -0.1875 to 0.1875
Outputs:
- new_states: float32 [3, 38912, 1792], P(None, ('dp', 'fsdp'))
- activations: bfloat16 [4096, 14336], P('fsdp', 'dp')
The draws below stay inside these ranges and needn't reach their ends.
Inputs may be any that keep to these rules, and one draw needn't show every extreme that they name: Each row starts at 0, ends at 4096 and rises; old_bounds[g, f] is within 8 of f * 256, so each piece has 240 to 272 rows, and 272 is reached in every group. `new_bounds`: each row starts at 0 and ends at 4096; every entry is within 16 of the same entry of old_bounds, each piece has at most 304 rows, and 304 is reached in every group. `failed`: every group appears exactly 16 // 8 times. `old_states`: copy 0 of a failed device holds nothing of the states; the third state is positive.
All inputs are finite; a program needn't handle non-finite values.
Results may differ from the reference program's by a relative error of at most 0.018.
Values may be sent and summed in bfloat16 or wider, within the bound.
A program may use at most 192 MiB of HBM per device.

```python
import math
import jax
import jax.numpy as jnp
from jax import lax

D = 4096
F = 14336
TOK = 256
TOKENS = 4096
FB = 1792
R = 256
M = 16
CAPO = 272
CAPN = 304
N_DP = 8
N_FSDP = 16


def bound_tables(key):
    base = jax.random.fold_in(key, 7)
    key_one, key_two, key_three, key_four = jax.random.split(base, 4)
    half_margin = M // 2
    columns = jnp.arange(N_FSDP + 1, dtype=jnp.int32)[None, :]
    widest = jax.random.randint(key_two, (N_DP, 1), 1, N_FSDP - 1)
    ends = (columns == 0) | (columns == N_FSDP)
    jitter = jax.random.randint(key_one, (N_DP, N_FSDP + 1), -half_margin, half_margin + 1)
    jitter = jnp.where(columns == widest, -half_margin, jitter)
    jitter = jnp.where(columns == widest + 1, half_margin, jitter)
    jitter = jnp.where(ends, 0, jitter)
    old_cut = columns * R + jitter
    moves_by = jax.random.randint(key_three, (N_DP, N_FSDP + 1), -M, M + 1)
    moves_by = jnp.where(columns == widest, -M, moves_by)
    moves_by = jnp.where(columns == widest + 1, M, moves_by)
    moves_by = jnp.where(ends, 0, moves_by)
    new_cut = old_cut + moves_by
    evenly = jnp.arange(N_FSDP, dtype=jnp.int32) % N_DP
    lost_groups = jax.random.permutation(key_four, evenly)
    return (old_cut.astype(jnp.int32), new_cut.astype(jnp.int32), lost_groups.astype(jnp.int32))


def state_draw(key):
    key_one, key_two, key_three = jax.random.split(key, 3)
    array_shape = (N_DP, N_FSDP, CAPO, FB)
    weight = jnp.clip(jax.random.normal(key_one, array_shape), -4.0, 4.0) / math.sqrt(D)
    moment = 0.3 * jnp.clip(jax.random.normal(key_two, array_shape), -4.0, 4.0)
    second = jnp.exp(jax.random.uniform(jax.random.fold_in(key_three, 3), array_shape, minval=math.log(0.001), maxval=0.0))
    return jnp.stack([weight, moment, second]).astype(jnp.float32)


def draw_old_bounds(key, part):
    return bound_tables(key)[0]


def draw_new_bounds(key, part):
    return bound_tables(key)[1]


def draw_failed(key, part):
    return bound_tables(key)[2]


def draw_old_states(key, part):
    lost_groups = bound_tables(key)[2]
    base = jax.random.fold_in(key, 11)
    own_copy = state_draw(jax.random.fold_in(base, 1))
    saved_copy = state_draw(jax.random.fold_in(base, 2))
    spare_one = state_draw(jax.random.fold_in(base, 3))
    is_lost = (jnp.arange(N_DP, dtype=jnp.int32)[:, None] == lost_groups[None, :])[None, :, :, None, None]
    first_copy = jnp.where(is_lost, spare_one, own_copy)
    return jnp.stack([first_copy, saved_copy], 1).reshape(3, 2, N_DP * N_FSDP * CAPO, FB)


def shard_levels(key, extent, cuts, low, largest):
    gain = 1.0
    for position, blocks in cuts:
        steps = jax.random.uniform(jax.random.fold_in(jax.random.fold_in(key, 6), position), (blocks,), jnp.float32, low / len(cuts), largest / len(cuts))
        gain = gain * jnp.repeat(jnp.exp(steps), extent[position] // blocks).reshape((-1,) + (1,) * (len(extent) - 1 - position))
    return gain


def gaussian(own_key, dims, scale, limit, pieces=(), kind=jnp.bfloat16):
    level = shard_levels(own_key, dims, pieces, -0.22, 0.18) if pieces else 1.0
    drawn = jax.random.normal(own_key, dims, jnp.float32) * scale * level
    return jnp.minimum(jnp.maximum(drawn, -limit), limit).astype(kind)


def setup_inputs(seed: int = 0) -> dict:
    key_of = jax.random.split(jax.random.key(seed), 7)
    return {
        "old_states": draw_old_states(jax.random.fold_in(key_of[6], 71), 0),
        "old_bounds": draw_old_bounds(jax.random.fold_in(key_of[6], 71), 0),
        "new_bounds": draw_new_bounds(jax.random.fold_in(key_of[6], 71), 0),
        "failed": draw_failed(jax.random.fold_in(key_of[6], 71), 0),
        "tokens": gaussian(key_of[4], (TOKENS, D), 1.0, 6.0, ((0, 16),)),
        "cotangent": gaussian(key_of[5], (TOKENS, F), (2.0 / TOKENS ** 0.5), 0.1875, ((0, 16), (1, 8))),
    }


beta_one = 0.9
beta_two = 0.95
learn_rate = 0.01
decay_rate = 0.1
epsilon = 1e-08
correct_one = 1.0 - 0.9 ** 8
correct_two = 1.0 - 0.95 ** 8

def reference(old_states, old_bounds, new_bounds, failed, tokens, cotangent):
    row_ids = jnp.arange(D, dtype=jnp.int32)
    slot_ids = jnp.arange(N_FSDP * CAPN, dtype=jnp.int32)

    def one_group(group_id):
        bounds = old_bounds[group_id]
        member_id = lax.optimization_barrier(jnp.sum((row_ids[:, None] >= bounds[None, 1:N_FSDP]).astype(jnp.int32), axis=1))
        is_lost = jnp.take(failed, member_id) == group_id
        holder = jnp.where(is_lost, (group_id + N_DP - 1) % N_DP, group_id).astype(jnp.int32)
        offset = row_ids - jnp.take(bounds, member_id)
        flat_index = ((holder * N_FSDP + member_id) * CAPO + offset).astype(jnp.int32)
        gathered = jnp.take(old_states, flat_index, axis=2)
        block_rows = jnp.where(is_lost[None, :, None], gathered[:, 1], gathered[:, 0])
        weight = block_rows[0]
        hidden = jnp.dot(tokens, weight.astype(jnp.bfloat16), preferred_element_type=jnp.float32).astype(jnp.bfloat16)
        cot_block = lax.dynamic_slice_in_dim(cotangent, (group_id * FB).astype(jnp.int32), FB, 1)

        def add_part(running, member):
            token_rows = lax.dynamic_slice_in_dim(tokens, (member * TOK).astype(jnp.int32), TOK, 0)
            cot_rows = lax.dynamic_slice_in_dim(cot_block, (member * TOK).astype(jnp.int32), TOK, 0)
            part_sum = jnp.dot(token_rows.T, cot_rows, preferred_element_type=jnp.float32)
            rounded = lax.optimization_barrier(part_sum.astype(jnp.bfloat16))
            return (running + rounded.astype(jnp.float32), None)
        gradient, _ = lax.scan(add_part, jnp.zeros((D, FB), jnp.float32), jnp.arange(N_FSDP, dtype=jnp.int32))
        moment_one = beta_one * block_rows[1] + (1.0 - beta_one) * gradient
        moment_two = beta_two * block_rows[2] + (1.0 - beta_two) * gradient * gradient
        update_dir = moment_one / correct_one / (jnp.sqrt(moment_two / correct_two) + epsilon) + decay_rate * weight
        new_weight = weight - learn_rate * update_dir
        updated = jnp.stack([new_weight, moment_one, moment_two])
        cuts = new_bounds[group_id]
        owner_ids = slot_ids // CAPN
        offsets = slot_ids % CAPN
        first_row = jnp.take(cuts, owner_ids)
        length = jnp.take(cuts, owner_ids + 1) - first_row
        target = jnp.minimum(first_row + offsets, D - 1).astype(jnp.int32)
        placed = jnp.take(updated, target, axis=1)
        placed = jnp.where((offsets < length)[None, :, None], placed, jnp.zeros((), jnp.float32))
        return (placed, hidden)
    placed, hidden = lax.map(one_group, jnp.arange(N_DP, dtype=jnp.int32))
    new_states = jnp.transpose(placed, (1, 0, 2, 3)).reshape(3, N_DP * N_FSDP * CAPN, FB)
    activations = jnp.transpose(hidden, (1, 0, 2)).reshape(TOKENS, N_DP * FB)
    return (new_states, activations)
```

```python
import jax
import jax.numpy as jnp
from jax import lax
from jax.experimental import pallas as pl
from jax.experimental.pallas import tpu as pltpu
from jax.sharding import PartitionSpec as P

beta_one = 0.9
beta_two = 0.95
learn_rate = 0.01
decay_rate = 0.1
epsilon = 1e-08
correct_one = 1.0 - 0.9**8
correct_two = 1.0 - 0.95**8

MESH = pl.DeviceIdType.MESH
SIDE = 4
ROWS = 256
NEAR = 8
FAR = 24
MOVE = 16
SHORT = ROWS - 2 * NEAR
OLD = ROWS + 2 * NEAR
NEW = ROWS + 2 * FAR
CUT = 256
DEPTH = 1152
TALL = 1088
W_HALF = 144
G_HALF = 160
A_HALF = 128
BF = jnp.bfloat16
F32 = jnp.float32


def rows_of(count):
    return lax.broadcasted_iota(jnp.int32, (count, CUT), 0)


def rows_from(ref, start, count):
    base = pl.multiple_of((start // 8) * 8, 8)
    rest = start - base
    tiles = ref[pl.ds(base, count + 8), :].reshape(count // 8 + 1, 8, CUT)
    turned = pltpu.roll(tiles, lax.rem(8 - rest, 8), 1)
    inner = lax.broadcasted_iota(jnp.int32, (count // 8, 8, CUT), 1)
    return jnp.where(inner < 8 - rest, turned[:-1], turned[1:]).reshape(count, CUT)


def prepare(old_bounds, failed, states, w_own, w_back, m_back, r_own, r_back, pad):
    group, member = lax.axis_index("dp"), lax.axis_index("fsdp")
    following = lax.rem(group + 1, lax.axis_size("dp"))
    lost = failed[member]
    slot = rows_of(OLD)
    for copy, owner, keep, window, rims in (
        (0, group, lost != group, w_own, r_own),
        (1, following, lost == following, w_back, r_back),
    ):
        start = old_bounds[owner, member]
        length = old_bounds[owner, member + 1] - start
        shift = start - ROWS * member + NEAR
        usable = jnp.where(keep, length, 0)
        some = rows_of(MOVE) < usable
        for state in range(3):
            value = states[state, copy]
            pad[state, MOVE : MOVE + OLD] = value
            if state == 0:
                moved = rows_from(pad.at[state], MOVE - shift, OLD)
                place = slot - shift
                window[0] = jnp.where((place >= 0) & (place < usable), moved, 0.0).astype(BF)
            elif copy == 1:
                m_back[0, state - 1] = value.astype(BF)
            rims[0, 0, state] = jnp.where(some, value[:MOVE], 0.0).astype(BF)
            rims[1, 0, state] = jnp.where(some, rows_from(pad.at[state], length, MOVE), 0.0).astype(BF)


def update(old_bounds, new_bounds, failed, states, w_back, m_back, rims, gradient, out, ext, g_pad, w_pad, r_pad):
    group, member = lax.axis_index("dp"), lax.axis_index("fsdp")
    lost = failed[member] == group
    old_start = old_bounds[group, member]
    old_len = old_bounds[group, member + 1] - old_start
    new_start = new_bounds[group, member]
    new_len = new_bounds[group, member + 1] - new_start
    step = new_start - old_start
    from_back = jnp.where(lost, old_len, 0)
    slot = rows_of(OLD)
    w_pad[:OLD] = w_back[0].astype(F32)
    moved = []
    for state in range(3):
        if state == 0:
            back = rows_from(w_pad, old_start - ROWS * member + NEAR, OLD)
        else:
            back = m_back[0, state - 1].astype(F32)
        value = jnp.where(slot < from_back, back, states[state, 0])
        r_pad[: 2 * MOVE] = jnp.zeros((2 * MOVE, CUT), F32)
        r_pad[2 * MOVE : 3 * MOVE] = rims[0, 0, state].astype(F32)
        r_pad[3 * MOVE :] = jnp.zeros((3 * MOVE + 8, CUT), F32)
        late = rows_from(r_pad, 2 * MOVE - (old_len - SHORT), 3 * MOVE)
        ext[state, :MOVE] = rims[1, 0, state].astype(F32)
        value = jnp.where(slot < old_len, value, 0.0)
        ext[state, MOVE : MOVE + SHORT] = value[:SHORT]
        ext[state, MOVE + SHORT : MOVE + OLD] = value[SHORT:] + late[: OLD - SHORT]
        ext[state, MOVE + OLD : MOVE + OLD + MOVE] = late[OLD - SHORT :]
        moved.append(rows_from(ext.at[state], MOVE + step, NEW))
    g_pad[:NEW] = gradient[0]
    grad = rows_from(g_pad, new_start - ROWS * member + FAR, NEW)
    weight, one, two = moved
    one = beta_one * one + (1.0 - beta_one) * grad
    two = beta_two * two + (1.0 - beta_two) * grad * grad
    direction = one / correct_one / (jnp.sqrt(two / correct_two) + epsilon) + decay_rate * weight
    here = rows_of(NEW) < new_len
    out[0] = jnp.where(here, weight - learn_rate * direction, 0.0)
    out[1] = jnp.where(here, one, 0.0)
    out[2] = jnp.where(here, two, 0.0)


def exchange(
    count,
    tokens, cot, w_own, w_back, m_back, r_own, r_back,
    act, grad, w_out, m_out, rims_out,
    tok, tok_t, cots, ws, wk, w_mine, w_arr, r_mine, r_arr,
    g_all, a_all, g_opp, g_opp_in, g_side, g_side_in, a_opp, a_opp_in, a_side, a_side_in, g_fin, a_fin,
    send, recv, local, tok_send, tok_recv, mate_send, mate_recv, w_send, w_recv, misc_send, misc_recv, misc_local,
):
    dp, member = lax.axis_index("dp"), lax.axis_index("fsdp")
    groups, members = lax.axis_size("dp"), lax.axis_size("fsdp")
    y, z = member // SIDE, lax.rem(member, SIDE)
    core = lax.rem(dp, 2)
    y_to = [{"fsdp": lax.rem(y + r, SIDE) * SIDE + z} for r in range(SIDE)]
    z_to = [{"fsdp": y * SIDE + lax.rem(z + r, SIDE)} for r in range(SIDE)]
    following, preceding = {"dp": lax.rem(dp + 1, groups)}, {"dp": lax.rem(dp + groups - 1, groups)}
    mate = {"dp": dp + 1 - 2 * core}
    f_up, f_down = {"fsdp": lax.rem(member + 1, members)}, {"fsdp": lax.rem(member + members - 1, members)}

    barrier = pltpu.get_barrier_semaphore()
    peers = y_to[1:] + [z_to[1], z_to[3], following, preceding, mate, f_up, f_down]
    for peer in peers:
        pl.semaphore_signal(barrier, inc=1, device_id=peer, device_id_type=MESH)
    pl.semaphore_wait(barrier, len(peers))

    def remote(src, dst, ssem, rsem, peer):
        return pltpu.make_async_remote_copy(
            src_ref=src, dst_ref=dst, send_sem=ssem, recv_sem=rsem, device_id=peer, device_id_type=MESH
        )

    def columns(c):
        return pl.ds(pl.multiple_of(c * CUT, CUT), CUT)

    half = pl.ds(pl.multiple_of(core * (ROWS // 2), ROWS // 2), ROWS // 2)
    other = pl.ds(pl.multiple_of((1 - core) * (ROWS // 2), ROWS // 2), ROWS // 2)

    def tok_copy(r):
        place = pl.ds(pl.multiple_of(lax.rem(y + r, SIDE) * (SIDE * ROWS), SIDE * ROWS), DEPTH)
        return remote(tokens.at[half, place], tok.at[SIDE - r, half], tok_send.at[r], tok_recv.at[r], y_to[r])

    def mate_copy(r):
        return remote(tok.at[SIDE - r, half], tok.at[SIDE - r, half], mate_send.at[r], mate_recv.at[r], mate)

    def w_copy(c):
        return remote(w_back.at[c], w_arr.at[c], w_send.at[c], w_recv.at[c], following)

    def misc(k):
        if k == 0:
            return remote(r_back, r_arr, misc_send.at[0], misc_recv.at[0], following)
        if k == 1:
            return remote(m_back, m_out, misc_send.at[1], misc_recv.at[1], following)
        if k == 2:
            return remote(r_mine.at[0], rims_out.at[0], misc_send.at[2], misc_recv.at[2], f_down)
        return remote(r_mine.at[1], rims_out.at[1], misc_send.at[3], misc_recv.at[3], f_up)

    def copy(kind, c):
        src, dst, peer = {
            0: (lambda: (ws.at[c, 0], ws.at[c, 3], z_to[1])),
            1: (lambda: (ws.at[c, 0], ws.at[c, 1], z_to[3])),
            2: (lambda: (ws.at[c, 3, :W_HALF], ws.at[c, 2, :W_HALF], z_to[1])),
            3: (lambda: (ws.at[c, 1, W_HALF:], ws.at[c, 2, W_HALF:], z_to[3])),
            4: (lambda: (cot.at[:, columns(c)], cots.at[c, 3], y_to[1])),
            5: (lambda: (cot.at[:, columns(c)], cots.at[c, 1], y_to[3])),
            6: (lambda: (cots.at[c, 3, :A_HALF], cots.at[c, 2, :A_HALF], y_to[1])),
            7: (lambda: (cots.at[c, 1, A_HALF:], cots.at[c, 2, A_HALF:], y_to[3])),
            8: (lambda: (g_opp.at[c, :G_HALF], g_opp_in.at[c, :G_HALF], z_to[1])),
            9: (lambda: (g_opp.at[c, G_HALF:], g_opp_in.at[c, G_HALF:], z_to[3])),
            10: (lambda: (g_side.at[c, 0], g_side_in.at[c, 0], z_to[1])),
            11: (lambda: (g_side.at[c, 1], g_side_in.at[c, 1], z_to[3])),
            12: (lambda: (a_opp.at[c, :A_HALF], a_opp_in.at[c, :A_HALF], y_to[1])),
            13: (lambda: (a_opp.at[c, A_HALF:], a_opp_in.at[c, A_HALF:], y_to[3])),
            14: (lambda: (a_side.at[c, 0], a_side_in.at[c, 0], y_to[1])),
            15: (lambda: (a_side.at[c, 1], a_side_in.at[c, 1], y_to[3])),
        }[kind]()
        return remote(src, dst, send.at[kind, c], recv.at[kind, c], peer)

    def here(k, c):
        src, dst = {
            0: (lambda: (cot.at[:, columns(c)], cots.at[c, 0])),
            1: (lambda: (g_fin.at[c], grad.at[c])),
            2: (lambda: (a_fin.at[c], act.at[:, columns(c)])),
            3: (lambda: (w_arr.at[c], w_out.at[c])),
        }[k]()
        return pltpu.make_async_copy(src, dst, local.at[k, c])

    def mine(k):
        own = pl.ds(pl.multiple_of(y * (SIDE * ROWS), SIDE * ROWS), DEPTH)
        src, dst = ((w_own, w_mine), (r_own, r_mine), (tokens.at[:, own], tok.at[0]))[k]
        return pltpu.make_async_copy(src, dst, misc_local.at[k])

    for r in (1, 3, 2):
        tok_copy(r).start()
    misc(0).start()

    @pl.loop(0, count)
    def _(c):
        w_copy(c).start()
        here(0, c).start()

    for k in range(3):
        mine(k).start()
    misc(1).start()
    wk[: 2 * NEAR] = jnp.zeros((2 * NEAR, CUT), BF)
    wk[SIDE * ROWS + 2 * MOVE :] = jnp.zeros((DEPTH - SIDE * ROWS - 2 * MOVE, CUT), BF)
    mine(0).wait()

    def gather(c):
        copy(4, c).start()
        copy(5, c).start()
        w_copy(c).wait_recv()
        here(3, c).start()
        ws[c, 0] = w_mine[c] + w_arr[c]
        copy(0, c).start()
        copy(1, c).start()

    def hand_on(c):
        for kind in (0, 1, 4, 5):
            copy(kind, c).wait_recv()
            copy(kind + 2, c).start()

    def multiply(c):
        slot = lax.rem(c, 3)
        here(0, c).wait()
        copy(6, c).wait_recv()
        copy(7, c).wait_recv()

        @pl.loop(0, TALL // OLD)
        def _(i):
            rows = pl.ds(pl.multiple_of(i * OLD, 16), OLD)
            g_all[slot, rows] = jnp.dot(
                tok_t[rows], cots[c].reshape(SIDE * ROWS, CUT), preferred_element_type=F32
            )

        far = pl.ds(pl.multiple_of(lax.rem(z + 2, SIDE) * ROWS, ROWS), NEW)
        g_opp[c] = g_all[slot, far].astype(BF)
        copy(8, c).start()
        copy(9, c).start()
        copy(2, c).wait_recv()
        copy(3, c).wait_recv()
        for p in range(SIDE):
            source = lax.rem(p - z + SIDE, SIDE)
            at = ROWS * p + MOVE
            if p == 0:
                wk[at : at + MOVE] = ws[c, source, :MOVE]
            else:
                wk[at : at + MOVE] = wk[at : at + MOVE] + ws[c, source, :MOVE]
            wk[at + MOVE : at + OLD] = ws[c, source, MOVE:]

        @pl.loop(0, SIDE)
        def _(r):
            a_all[slot, r] = jnp.dot(tok[r], wk[...], preferred_element_type=F32)

        a_opp[c] = a_all[slot, 2].astype(BF)
        copy(12, c).start()
        copy(13, c).start()

    def add_on(c):
        slot = lax.rem(c, 3)
        copy(8, c).wait_recv()
        copy(9, c).wait_recv()
        up = pl.multiple_of(lax.rem(z + 1, SIDE) * ROWS, ROWS)
        down = pl.multiple_of(lax.rem(z + 3, SIDE) * ROWS, ROWS)
        g_side[c, 0, :G_HALF] = (g_all[slot, pl.ds(up, G_HALF)] + g_opp_in[c, :G_HALF].astype(F32)).astype(BF)
        g_side[c, 0, G_HALF:] = g_all[slot, pl.ds(up + G_HALF, NEW - G_HALF)].astype(BF)
        g_side[c, 1, :G_HALF] = g_all[slot, pl.ds(down, G_HALF)].astype(BF)
        g_side[c, 1, G_HALF:] = (
            g_all[slot, pl.ds(down + G_HALF, NEW - G_HALF)] + g_opp_in[c, G_HALF:].astype(F32)
        ).astype(BF)
        copy(10, c).start()
        copy(11, c).start()
        copy(12, c).wait_recv()
        copy(13, c).wait_recv()
        a_side[c, 0, :A_HALF] = (a_all[slot, 1, :A_HALF] + a_opp_in[c, :A_HALF].astype(F32)).astype(BF)
        a_side[c, 0, A_HALF:] = a_all[slot, 1, A_HALF:].astype(BF)
        a_side[c, 1, :A_HALF] = a_all[slot, 3, :A_HALF].astype(BF)
        a_side[c, 1, A_HALF:] = (a_all[slot, 3, A_HALF:] + a_opp_in[c, A_HALF:].astype(F32)).astype(BF)
        copy(14, c).start()
        copy(15, c).start()

    def finish(c):
        slot = lax.rem(c, 3)
        copy(10, c).wait_recv()
        copy(11, c).wait_recv()
        rows = pl.ds(pl.multiple_of(z * ROWS, ROWS), NEW)
        g_fin[c] = g_all[slot, rows] + g_side_in[c, 0].astype(F32) + g_side_in[c, 1].astype(F32)
        here(1, c).start()
        copy(14, c).wait_recv()
        copy(15, c).wait_recv()
        a_fin[c] = (a_all[slot, 0] + a_side_in[c, 0].astype(F32) + a_side_in[c, 1].astype(F32)).astype(BF)
        here(2, c).start()

    gather(0)
    for r in (1, 3, 2):
        tok_copy(r).wait_recv()
        mate_copy(r).start()
    gather(1)
    hand_on(0)

    mine(1).wait()
    misc(0).wait_recv()
    r_mine[...] = r_mine[...] + r_arr[...]
    misc(2).start()
    misc(3).start()

    mine(2).wait()
    tok_t[:, :ROWS] = tok[0].T
    for r in (1, 3, 2):
        mate_copy(r).wait_recv()
        k = SIDE - r
        tok_t[:, ROWS * k : ROWS * (k + 1)] = tok[k].T

    @pl.loop(2, count + 4)
    def _(t):
        @pl.when(t < count)
        def _():
            gather(t)

        @pl.when(t < count + 1)
        def _():
            hand_on(t - 1)

        @pl.when((t >= 3) & (t < count + 3))
        def _():
            add_on(t - 3)

        @pl.when(t < count + 2)
        def _():
            multiply(t - 2)

        @pl.when(t >= 4)
        def _():
            finish(t - 4)

    @pl.loop(0, count)
    def _(c):
        for kind in range(16):
            copy(kind, c).wait_send()
        w_copy(c).wait_send()
        for k in (1, 2, 3):
            here(k, c).wait()

    for r in (1, 2, 3):
        tok_copy(r).wait_send()
        mate_copy(r).wait_send()
    misc(0).wait_send()
    for k in (1, 2, 3):
        misc(k).wait()


def body(old_states, old_bounds, new_bounds, failed, tokens, cotangent):
    width = cotangent.shape[1]
    count = width // CUT
    smem = pl.BlockSpec(memory_space=pltpu.SMEM)
    hbm = pl.BlockSpec(memory_space=pl.ANY)
    shape = jax.ShapeDtypeStruct
    wide = shape((count, OLD, CUT), BF)
    two_wide = shape((count, 2, OLD, CUT), BF)
    rim = shape((2, count, 3, MOVE, CUT), BF)
    wide_spec = pl.BlockSpec((1, OLD, CUT), lambda i: (i, 0, 0))
    two_spec = pl.BlockSpec((1, 2, OLD, CUT), lambda i: (i, 0, 0, 0))
    rim_spec = pl.BlockSpec((2, 1, 3, MOVE, CUT), lambda i: (0, i, 0, 0, 0))

    w_own, w_back, m_back, r_own, r_back = pl.pallas_call(
        prepare,
        grid=(count,),
        in_specs=[smem, smem, pl.BlockSpec((3, 2, OLD, CUT), lambda i: (0, 0, 0, i))],
        out_specs=[wide_spec, wide_spec, two_spec, rim_spec, rim_spec],
        out_shape=[wide, wide, two_wide, rim, rim],
        scratch_shapes=[pltpu.VMEM((3, OLD + 2 * MOVE + 8, CUT), F32)],
        name="prepare",
    )(old_bounds, failed, old_states)

    padded = jnp.pad(tokens, ((0, 0), (FAR, DEPTH - SIDE * ROWS - FAR)))
    vm = pltpu.VMEM
    dma = pltpu.SemaphoreType.DMA
    act, grad, w_arr, m_arr, rims = pl.pallas_call(
        lambda *refs: exchange(count, *refs),
        in_specs=[hbm] * 7,
        out_specs=[hbm] * 5,
        out_shape=[
            shape((ROWS, width), BF),
            shape((count, NEW, CUT), F32),
            wide,
            two_wide,
            rim,
        ],
        scratch_shapes=[
            vm((SIDE, ROWS, DEPTH), BF),
            vm((DEPTH, SIDE * ROWS), BF),
            vm((count, SIDE, ROWS, CUT), BF),
            vm((count, SIDE, OLD, CUT), BF),
            vm((DEPTH, CUT), BF),
            vm((count, OLD, CUT), BF),
            vm((count, OLD, CUT), BF),
            vm((2, count, 3, MOVE, CUT), BF),
            vm((2, count, 3, MOVE, CUT), BF),
            vm((3, TALL, CUT), F32),
            vm((3, SIDE, ROWS, CUT), F32),
            vm((count, NEW, CUT), BF),
            vm((count, NEW, CUT), BF),
            vm((count, 2, NEW, CUT), BF),
            vm((count, 2, NEW, CUT), BF),
            vm((count, ROWS, CUT), BF),
            vm((count, ROWS, CUT), BF),
            vm((count, 2, ROWS, CUT), BF),
            vm((count, 2, ROWS, CUT), BF),
            vm((count, NEW, CUT), F32),
            vm((count, ROWS, CUT), BF),
            dma((16, count)),
            dma((16, count)),
            dma((4, count)),
            dma((SIDE,)),
            dma((SIDE,)),
            dma((SIDE,)),
            dma((SIDE,)),
            dma((count,)),
            dma((count,)),
            dma((4,)),
            dma((4,)),
            dma((3,)),
        ],
        compiler_params=pltpu.CompilerParams(
            collective_id=0, has_side_effects=True, vmem_limit_bytes=50 * 2**20
        ),
        name="exchange",
    )(padded, cotangent, w_own, w_back, m_back, r_own, r_back)

    new_states = pl.pallas_call(
        update,
        grid=(count,),
        in_specs=[
            smem,
            smem,
            smem,
            pl.BlockSpec((3, 1, OLD, CUT), lambda i: (0, 0, 0, i)),
            wide_spec,
            two_spec,
            rim_spec,
            pl.BlockSpec((1, NEW, CUT), lambda i: (i, 0, 0)),
        ],
        out_specs=pl.BlockSpec((3, NEW, CUT), lambda i: (0, 0, i)),
        out_shape=shape((3, NEW, width), F32),
        scratch_shapes=[
            vm((3, NEW + 2 * MOVE + 8, CUT), F32),
            vm((NEW + 2 * FAR + 8, CUT), F32),
            vm((OLD + MOVE + 8, CUT), F32),
            vm((6 * MOVE + 8, CUT), F32),
        ],
        name="update",
    )(old_bounds, new_bounds, failed, old_states, w_arr, m_arr, rims, grad)
    return new_states, act


def solution(mesh):
    in_specs = (
        P(None, None, ("dp", "fsdp"), None),
        P(),
        P(),
        P(),
        P("fsdp", None),
        P("fsdp", "dp"),
    )
    out_specs = (P(None, ("dp", "fsdp"), None), P("fsdp", "dp"))
    return jax.shard_map(body, mesh=mesh, in_specs=in_specs, out_specs=out_specs, check_vma=False)
```

```python
import jax
import jax.numpy as jnp
from jax import lax
from jax.experimental import pallas as pl
from jax.experimental.pallas import tpu as pltpu
from jax.sharding import PartitionSpec as P

beta_one = 0.9
beta_two = 0.95
learn_rate = 0.01
decay_rate = 0.1
epsilon = 1e-08
correct_one = 1.0 - 0.9**8
correct_two = 1.0 - 0.95**8

MESH = pl.DeviceIdType.MESH
SIDE = 4
ROWS = 256
NEAR = 8
FAR = 24
MOVE = 16
SHORT = ROWS - 2 * NEAR
OLD = ROWS + 2 * NEAR
NEW = ROWS + 2 * FAR
CUT = 256
SPARE = 64
LANE = 128
DEPTH = SIDE * ROWS + 2 * LANE
SKIP = 96
TALL = 1088
W_HALF = 144
G_HALF = 160
A_HALF = 128
PRE = 5
AHEAD = 3
HAND = 1
MOM = 1
ADD = 2
END = 4
LOAD = 2
RING = END + 1
BF = jnp.bfloat16
F32 = jnp.float32


def rows_of(count):
    return lax.broadcasted_iota(jnp.int32, (count, CUT), 0)


def rows_from(ref, start, count, coarse):
    tiles = ref[: count + 8 + sum(coarse), :].reshape(count // 8 + 1 + sum(coarse) // 8, 8, CUT)
    amount = jnp.broadcast_to(start, (1, 8, CUT))
    for bit in coarse:
        tiles = jnp.where((amount & bit) > 0, tiles[bit // 8 :], tiles[: -(bit // 8)])
    for bit in (1, 2, 4):
        tiles = jnp.where((amount & bit) > 0, pltpu.roll(tiles, 8 - bit, 1), tiles)
    inner = lax.broadcasted_iota(jnp.int32, (1, 8, CUT), 1)
    return jnp.where(inner < 8 - (amount & 7), tiles[:-1], tiles[1:]).reshape(count, CUT)


def exchange(
    count,
    old_bounds, new_bounds, failed, states, tokens, cot,
    new_states, act,
    w_in, m_in, ext, e_head, e_tail,
    tok, tok_t, cots, ws, wk_wide, wk, w_mine, w_back, w_arr, m_back, m_arr, r_mine, r_back, r_arr, rims,
    g_all, a_all, g_opp, g_opp_in, g_side, g_side_in, a_opp, a_opp_in, a_side, a_side_in, a_fin, out, g_pad, w_pad, r_pad,
    send, recv, local, tok_send, tok_recv, mate_send, mate_recv, dp_send, dp_recv, misc_send, misc_recv, misc_local,
):
    dp, member = lax.axis_index("dp"), lax.axis_index("fsdp")
    groups, members = lax.axis_size("dp"), lax.axis_size("fsdp")
    y, z = member // SIDE, lax.rem(member, SIDE)
    core = lax.rem(dp, 2)
    y_to = [{"fsdp": lax.rem(y + r, SIDE) * SIDE + z} for r in range(SIDE)]
    z_to = [{"fsdp": y * SIDE + lax.rem(z + r, SIDE)} for r in range(SIDE)]
    next_group = lax.rem(dp + 1, groups)
    following, preceding = {"dp": next_group}, {"dp": lax.rem(dp + groups - 1, groups)}
    mate = {"dp": dp + 1 - 2 * core}
    f_up, f_down = {"fsdp": lax.rem(member + 1, members)}, {"fsdp": lax.rem(member + members - 1, members)}

    barrier = pltpu.get_barrier_semaphore()
    peers = y_to[1:] + [z_to[1], z_to[3], following, preceding, mate, f_up, f_down]
    for peer in peers:
        pl.semaphore_signal(barrier, inc=1, device_id=peer, device_id_type=MESH)

    def remote(src, dst, ssem, rsem, peer):
        return pltpu.make_async_remote_copy(
            src_ref=src, dst_ref=dst, send_sem=ssem, recv_sem=rsem, device_id=peer, device_id_type=MESH
        )

    def columns(c):
        return pl.ds(pl.multiple_of(c * CUT, CUT), CUT)

    half = pl.ds(pl.multiple_of(core * (ROWS // 2), ROWS // 2), ROWS // 2)

    def parts(owner):
        span = SIDE * ROWS
        whole = span * SIDE
        begin = pl.multiple_of(owner * span, span)
        before = pl.multiple_of(lax.rem(owner * span + whole - LANE, whole), LANE)
        after = pl.multiple_of(lax.rem(owner * span + span, whole), LANE)
        return (
            (pl.ds(begin, span), pl.ds(LANE, span)),
            (pl.ds(before, LANE), pl.ds(0, LANE)),
            (pl.ds(after, LANE), pl.ds(LANE + span, LANE)),
        )

    def tok_copy(r, k):
        source, target = parts(lax.rem(y + r, SIDE))[k]
        return remote(
            tokens.at[half, source], tok.at[SIDE - r, half, target], tok_send.at[r, k], tok_recv.at[r, k], y_to[r]
        )

    def mate_copy(r):
        return remote(tok.at[SIDE - r, half], tok.at[SIDE - r, half], mate_send.at[r], mate_recv.at[r], mate)

    def w_copy(c):
        return remote(w_back.at[c], w_arr.at[c], dp_send.at[0, c], dp_recv.at[0, c], following)

    def m_copy(c):
        return remote(m_back.at[c], m_arr.at[c], dp_send.at[1, c], dp_recv.at[1, c], following)

    def rim_copy(k):
        if k == 0:
            return remote(r_back, r_arr, misc_send.at[0], misc_recv.at[0], following)
        if k == 1:
            return remote(r_mine.at[0], rims.at[0], misc_send.at[1], misc_recv.at[1], f_down)
        return remote(r_mine.at[1], rims.at[1], misc_send.at[2], misc_recv.at[2], f_up)

    def copy(kind, c):
        src, dst, peer = {
            0: (lambda: (ws.at[c, 0], ws.at[c, 3], z_to[1])),
            1: (lambda: (ws.at[c, 0], ws.at[c, 1], z_to[3])),
            2: (lambda: (ws.at[c, 3, :W_HALF], ws.at[c, 2, :W_HALF], z_to[1])),
            3: (lambda: (ws.at[c, 1, W_HALF:], ws.at[c, 2, W_HALF:], z_to[3])),
            4: (lambda: (cot.at[:, columns(c)], cots.at[c, 3], y_to[1])),
            5: (lambda: (cot.at[:, columns(c)], cots.at[c, 1], y_to[3])),
            6: (lambda: (cots.at[c, 3, :A_HALF], cots.at[c, 2, :A_HALF], y_to[1])),
            7: (lambda: (cots.at[c, 1, A_HALF:], cots.at[c, 2, A_HALF:], y_to[3])),
            8: (lambda: (g_opp.at[c, :G_HALF], g_opp_in.at[c, :G_HALF], z_to[1])),
            9: (lambda: (g_opp.at[c, G_HALF:], g_opp_in.at[c, G_HALF:], z_to[3])),
            10: (lambda: (g_side.at[c, 0], g_side_in.at[c, 0], z_to[1])),
            11: (lambda: (g_side.at[c, 1], g_side_in.at[c, 1], z_to[3])),
            12: (lambda: (a_opp.at[c, :A_HALF], a_opp_in.at[c, :A_HALF], y_to[1])),
            13: (lambda: (a_opp.at[c, A_HALF:], a_opp_in.at[c, A_HALF:], y_to[3])),
            14: (lambda: (a_side.at[c, 0], a_side_in.at[c, 0], y_to[1])),
            15: (lambda: (a_side.at[c, 1], a_side_in.at[c, 1], y_to[3])),
        }[kind]()
        return remote(src, dst, send.at[kind, c], recv.at[kind, c], peer)

    def here(k, c):
        src, dst = {
            0: (lambda: (cot.at[:, columns(c)], cots.at[c, 0])),
            1: (lambda: (states.at[0, :, :, columns(c)], w_in.at[lax.rem(c, 3), :, MOVE : MOVE + OLD])),
            2: (lambda: (states.at[1:3, 1, :, columns(c)], m_in.at[lax.rem(c, 2)])),
            3: (lambda: (states.at[:, 0, :, columns(c)], ext.at[lax.rem(c, 3), :, MOVE : MOVE + OLD])),
            4: (lambda: (a_fin.at[c], act.at[:, columns(c)])),
            5: (lambda: (out.at[lax.rem(c, 3)], new_states.at[:, :, columns(c)])),
        }[k]()
        return pltpu.make_async_copy(src, dst, local.at[k, c])

    def mine(k):
        if k < 3:
            source, target = parts(y)[k]
            src, dst = tokens.at[:, source], tok.at[0, :, target]
        elif k == 3:
            src, dst = states.at[:, :, :MOVE], e_head
        else:
            src, dst = states.at[:, :, OLD - 3 * MOVE :], e_tail.at[:, :, : 3 * MOVE]
        return pltpu.make_async_copy(src, dst, misc_local.at[k])

    lost_group = failed[member]
    old_start = old_bounds[dp, member]
    old_len = old_bounds[dp, member + 1] - old_start
    new_start = new_bounds[dp, member]
    new_len = new_bounds[dp, member + 1] - new_start
    back_start = old_bounds[next_group, member]
    back_len = old_bounds[next_group, member + 1] - back_start
    mean_start = ROWS * member
    lost_use = old_len * (lost_group == dp).astype(jnp.int32)
    own_use = old_len - lost_use
    back_use = back_len * (lost_group == next_group).astype(jnp.int32)

    def window(ref, start, usable):
        shift = start - mean_start + NEAR
        place = rows_of(OLD) - shift
        return jnp.where((place >= 0) & (place < usable), rows_from(ref, MOVE - shift, OLD, (16, 8)), 0.0).astype(BF)

    def windows(c):
        slot = lax.rem(c, 3)
        here(1, c).wait()
        w_back[c] = window(w_in.at[slot, 1], back_start, back_use)
        w_copy(c).start()
        w_mine[c] = window(w_in.at[slot, 0], old_start, own_use)

        @pl.when(c + 3 < count)
        def _():
            here(1, c + 3).start()

    def rim_rows():
        mine(3).wait()
        mine(4).wait()
        row = rows_of(MOVE)

        @pl.loop(0, count)
        def _(c):
            for number, (length, usable, rim) in enumerate(((old_len, own_use, r_mine), (back_len, back_use, r_back))):
                some = row < usable
                for state in range(3):
                    head = e_head[state, number, :, columns(c)]
                    tail = rows_from(e_tail.at[state, number, :, columns(c)], length - SHORT, MOVE, (32, 16, 8))
                    rim[0, c, state] = jnp.where(some, head, 0.0).astype(BF)
                    rim[1, c, state] = jnp.where(some, tail, 0.0).astype(BF)

    def moments(c):
        here(2, c).wait()
        m_back[c] = m_in[lax.rem(c, 2)].astype(BF)
        m_copy(c).start()

        @pl.when(c + 2 < count)
        def _():
            here(2, c + 2).start()

    def gather(c):
        copy(4, c).start()
        copy(5, c).start()
        w_copy(c).wait_recv()
        ws[c, 0] = w_mine[c] + w_arr[c]
        copy(0, c).start()
        copy(1, c).start()

    def hand_on(c):
        for kind in (0, 1, 4, 5):
            copy(kind, c).wait_recv()
            copy(kind + 2, c).start()

    def multiply(c):
        slot = lax.rem(c, RING)
        here(0, c).wait()
        copy(6, c).wait_recv()
        copy(7, c).wait_recv()

        @pl.loop(0, TALL // OLD)
        def _(i):
            rows = pl.ds(pl.multiple_of(i * OLD, 16), OLD)
            taken = pl.ds(pl.multiple_of(i * OLD + SKIP, 16), OLD)
            g_all[slot, rows] = jnp.dot(
                tok_t[taken], cots[c].reshape(SIDE * ROWS, CUT), preferred_element_type=F32
            )

        far = pl.ds(pl.multiple_of(lax.rem(z + 2, SIDE) * ROWS + NEAR, NEAR), NEW)
        g_opp[c] = g_all[slot, far].astype(BF)
        copy(8, c).start()
        copy(9, c).start()
        copy(2, c).wait_recv()
        copy(3, c).wait_recv()
        for p in range(SIDE):
            source = lax.rem(p - z + SIDE, SIDE)
            at = LANE - NEAR + ROWS * p
            piece = ws[c, source].astype(F32)
            if p == 0:
                wk_wide[at : at + MOVE] = piece[:MOVE]
            else:
                wk_wide[at : at + MOVE] = wk_wide[at : at + MOVE] + piece[:MOVE]
            wk_wide[at + MOVE : at + OLD] = piece[MOVE:]
        wk[...] = wk_wide[...].astype(BF)

        @pl.loop(0, SIDE)
        def _(r):
            a_all[slot, r] = jnp.dot(tok[r], wk[...], preferred_element_type=F32)

        a_opp[c] = a_all[slot, 2].astype(BF)
        copy(12, c).start()
        copy(13, c).start()

    def add_on(c):
        slot = lax.rem(c, RING)
        copy(8, c).wait_recv()
        copy(9, c).wait_recv()
        up = pl.multiple_of(lax.rem(z + 1, SIDE) * ROWS + NEAR, NEAR)
        down = pl.multiple_of(lax.rem(z + 3, SIDE) * ROWS + NEAR, NEAR)
        g_side[c, 0, :G_HALF] = (g_all[slot, pl.ds(up, G_HALF)] + g_opp_in[c, :G_HALF].astype(F32)).astype(BF)
        g_side[c, 0, G_HALF:] = g_all[slot, pl.ds(up + G_HALF, NEW - G_HALF)].astype(BF)
        g_side[c, 1, :G_HALF] = g_all[slot, pl.ds(down, G_HALF)].astype(BF)
        g_side[c, 1, G_HALF:] = (
            g_all[slot, pl.ds(down + G_HALF, NEW - G_HALF)] + g_opp_in[c, G_HALF:].astype(F32)
        ).astype(BF)
        copy(10, c).start()
        copy(11, c).start()
        copy(12, c).wait_recv()
        copy(13, c).wait_recv()
        a_side[c, 0, :A_HALF] = (a_all[slot, 1, :A_HALF] + a_opp_in[c, :A_HALF].astype(F32)).astype(BF)
        a_side[c, 0, A_HALF:] = a_all[slot, 1, A_HALF:].astype(BF)
        a_side[c, 1, :A_HALF] = a_all[slot, 3, :A_HALF].astype(BF)
        a_side[c, 1, A_HALF:] = (a_all[slot, 3, A_HALF:] + a_opp_in[c, A_HALF:].astype(F32)).astype(BF)
        copy(14, c).start()
        copy(15, c).start()

    def finish(c):
        slot = lax.rem(c, RING)
        at = lax.rem(c, 3)
        row = rows_of(OLD)
        here(3, c).wait()
        m_copy(c).wait_recv()
        w_pad[:OLD] = w_arr[c].astype(F32)
        moved = []
        for state in range(3):
            if state == 0:
                back = rows_from(w_pad, old_start - mean_start + NEAR, OLD, (16, 8))
            else:
                back = m_arr[c, state - 1].astype(F32)
            r_pad[2 * MOVE : 3 * MOVE] = rims[0, c, state].astype(F32)
            late = rows_from(r_pad, 2 * MOVE - (old_len - SHORT), 3 * MOVE, (32, 16, 8))
            value = jnp.where(row < lost_use, back, ext[at, state, MOVE : MOVE + OLD])
            value = jnp.where(row < old_len, value, 0.0)
            ext[at, state, :MOVE] = rims[1, c, state].astype(F32)
            ext[at, state, MOVE : MOVE + SHORT] = value[:SHORT]
            ext[at, state, MOVE + SHORT : MOVE + OLD] = value[SHORT:] + late[: OLD - SHORT]
            ext[at, state, MOVE + OLD : MOVE + OLD + MOVE] = late[OLD - SHORT :]
            moved.append(rows_from(ext.at[at, state], MOVE + new_start - old_start, NEW, (32, 16, 8)))
        copy(14, c).wait_recv()
        copy(15, c).wait_recv()
        a_fin[c] = (a_all[slot, 0] + a_side_in[c, 0].astype(F32) + a_side_in[c, 1].astype(F32)).astype(BF)
        here(4, c).start()
        copy(10, c).wait_recv()
        copy(11, c).wait_recv()
        rows = pl.ds(pl.multiple_of(z * ROWS + NEAR, NEAR), NEW)
        g_pad[:NEW] = g_all[slot, rows] + g_side_in[c, 0].astype(F32) + g_side_in[c, 1].astype(F32)
        grad = rows_from(g_pad, new_start - mean_start + FAR, NEW, (32, 16, 8))
        weight, one, two = moved
        one = beta_one * one + (1.0 - beta_one) * grad
        two = beta_two * two + (1.0 - beta_two) * grad * grad
        direction = one / correct_one / (jnp.sqrt(two / correct_two) + epsilon) + decay_rate * weight
        inside = rows_of(NEW) < new_len

        @pl.when(c >= 3)
        def _():
            here(5, c - 3).wait()

        out[at, 0] = jnp.where(inside, weight - learn_rate * direction, 0.0)
        out[at, 1] = jnp.where(inside, one, 0.0)
        out[at, 2] = jnp.where(inside, two, 0.0)
        here(5, c).start()

    for c in range(3):
        here(1, c).start()
    for k in range(5):
        mine(k).start()
    for c in range(2):
        here(2, c).start()

    @pl.loop(0, count)
    def _(c):
        here(0, c).start()

    wk_wide[:LANE] = jnp.zeros((LANE, CUT), F32)
    wk_wide[LANE + SIDE * ROWS :] = jnp.zeros((LANE, CUT), F32)
    r_pad[...] = jnp.zeros(r_pad.shape, F32)
    pl.semaphore_wait(barrier, len(peers))
    for r in (1, 3, 2):
        for k in range(3):
            tok_copy(r, k).start()
    first = -PRE

    @pl.loop(0, count + END + PRE)
    def _(step):
        t = step + first

        @pl.when(t + PRE < count)
        def _():
            windows(t + PRE)

        @pl.when((t + AHEAD >= 0) & (t + AHEAD < count))
        def _():
            gather(t + AHEAD)

        @pl.when(t == -AHEAD)
        def _():
            rim_rows()
            rim_copy(0).start()

        @pl.when(t == 1 - AHEAD)
        def _():
            for r in (1, 3, 2):
                for k in range(3):
                    tok_copy(r, k).wait_recv()
                mate_copy(r).start()

        @pl.when((t + HAND >= 0) & (t + HAND < count))
        def _():
            hand_on(t + HAND)

        @pl.when((t + MOM >= 0) & (t + MOM < count))
        def _():
            moments(t + MOM)

        @pl.when(t == -1)
        def _():
            rim_copy(0).wait_recv()
            r_mine[...] = r_mine[...] + r_arr[...]
            rim_copy(1).start()
            rim_copy(2).start()
            for k in range(3):
                mine(k).wait()
            tok_t[:, :ROWS] = tok[0].T
            for r in (1, 3, 2):
                mate_copy(r).wait_recv()
                k = SIDE - r
                tok_t[:, ROWS * k : ROWS * (k + 1)] = tok[k].T

        @pl.when((t >= ADD) & (t < count + ADD))
        def _():
            add_on(t - ADD)

        @pl.when((t >= 0) & (t < count))
        def _():
            multiply(t)

        @pl.when((t >= END - LOAD) & (t < count + END - LOAD))
        def _():
            here(3, t - END + LOAD).start()

        @pl.when(t == END)
        def _():
            rim_copy(1).wait_recv()
            rim_copy(2).wait_recv()

        @pl.when(t >= END)
        def _():
            finish(t - END)

    @pl.loop(0, count)
    def _(c):
        for kind in range(16):
            copy(kind, c).wait_send()
        w_copy(c).wait_send()
        m_copy(c).wait_send()
        here(4, c).wait()

    for c in range(count - 3, count):
        here(5, c).wait()
    for r in (1, 2, 3):
        for k in range(3):
            tok_copy(r, k).wait_send()
        mate_copy(r).wait_send()
    for k in range(3):
        rim_copy(k).wait_send()


def body(old_states, old_bounds, new_bounds, failed, tokens, cotangent):
    width = cotangent.shape[1]
    count = width // CUT
    smem = pl.BlockSpec(memory_space=pltpu.SMEM)
    hbm = pl.BlockSpec(memory_space=pl.ANY)
    shape = jax.ShapeDtypeStruct
    vm = pltpu.VMEM
    dma = pltpu.SemaphoreType.DMA
    new_states, act = pl.pallas_call(
        lambda *refs: exchange(count, *refs),
        in_specs=[smem, smem, smem, hbm, hbm, hbm],
        out_specs=[hbm, hbm],
        out_shape=[shape((3, NEW, width), F32), shape((ROWS, width), BF)],
        scratch_shapes=[
            vm((3, 2, OLD + 2 * MOVE + 8, CUT), F32),
            vm((2, 2, OLD, CUT), F32),
            vm((3, 3, NEW + SPARE, CUT), F32),
            vm((3, 2, MOVE, width), F32),
            vm((3, 2, MOVE + SPARE, width), F32),
            vm((SIDE, ROWS, DEPTH), BF),
            vm((DEPTH, SIDE * ROWS), BF),
            vm((count, SIDE, ROWS, CUT), BF),
            vm((count, SIDE, OLD, CUT), BF),
            vm((DEPTH, CUT), F32),
            vm((DEPTH, CUT), BF),
            vm((count, OLD, CUT), BF),
            vm((count, OLD, CUT), BF),
            vm((count, OLD, CUT), BF),
            vm((count, 2, OLD, CUT), BF),
            vm((count, 2, OLD, CUT), BF),
            vm((2, count, 3, MOVE, CUT), BF),
            vm((2, count, 3, MOVE, CUT), BF),
            vm((2, count, 3, MOVE, CUT), BF),
            vm((2, count, 3, MOVE, CUT), BF),
            vm((RING, TALL, CUT), F32),
            vm((RING, SIDE, ROWS, CUT), F32),
            vm((count, NEW, CUT), BF),
            vm((count, NEW, CUT), BF),
            vm((count, 2, NEW, CUT), BF),
            vm((count, 2, NEW, CUT), BF),
            vm((count, ROWS, CUT), BF),
            vm((count, ROWS, CUT), BF),
            vm((count, 2, ROWS, CUT), BF),
            vm((count, 2, ROWS, CUT), BF),
            vm((count, ROWS, CUT), BF),
            vm((3, 3, NEW, CUT), F32),
            vm((NEW + SPARE, CUT), F32),
            vm((OLD + SPARE, CUT), F32),
            vm((3 * MOVE + SPARE, CUT), F32),
            dma((16, count)),
            dma((16, count)),
            dma((6, count)),
            dma((SIDE, 3)),
            dma((SIDE, 3)),
            dma((SIDE,)),
            dma((SIDE,)),
            dma((2, count)),
            dma((2, count)),
            dma((3,)),
            dma((3,)),
            dma((5,)),
        ],
        compiler_params=pltpu.CompilerParams(
            collective_id=0, has_side_effects=True, vmem_limit_bytes=60 * 2**20
        ),
        name="exchange",
    )(old_bounds, new_bounds, failed, old_states, tokens, cotangent)
    return new_states, act


def solution(mesh):
    in_specs = (
        P(None, None, ("dp", "fsdp"), None),
        P(),
        P(),
        P(),
        P("fsdp", None),
        P("fsdp", "dp"),
    )
    out_specs = (P(None, ("dp", "fsdp"), None), P("fsdp", "dp"))
    return jax.shard_map(body, mesh=mesh, in_specs=in_specs, out_specs=out_specs, check_vma=False)
```

```python
import jax
import jax.numpy as jnp
from jax import lax
from jax.experimental import pallas as pl
from jax.experimental.pallas import tpu as pltpu
from jax.sharding import PartitionSpec as P

beta_one = 0.9
beta_two = 0.95
learn_rate = 0.01
decay_rate = 0.1
epsilon = 1e-08
correct_one = 1.0 - 0.9**8
correct_two = 1.0 - 0.95**8

MESH = pl.DeviceIdType.MESH
SIDE = 4
ROWS = 256
NEAR = 8
FAR = 24
MOVE = 16
SHORT = ROWS - 2 * NEAR
OLD = ROWS + 2 * NEAR
NEW = ROWS + 2 * FAR
CUT = 256
SPARE = 64
LANE = 128
DEPTH = SIDE * ROWS + 2 * LANE
SKIP = 96
TALL = 1088
W_HALF = 144
G_HALF = 160
A_HALF = 128
PRE = 7
AHEAD = 5
HAND = 2
MOM = 1
TOK_ONE = -3
TOK_TWO = -1
TOK_END = 0
ADD = 2
END = 4
LOAD = 2
RING = END + 1
BF = jnp.bfloat16
F32 = jnp.float32


def rows_of(count):
    return lax.broadcasted_iota(jnp.int32, (count, CUT), 0)


def rows_from(ref, start, count, coarse):
    tiles = ref[: count + 8 + sum(coarse), :].reshape(count // 8 + 1 + sum(coarse) // 8, 8, CUT)
    amount = jnp.broadcast_to(start, (1, 8, CUT))
    for bit in coarse:
        tiles = jnp.where((amount & bit) > 0, tiles[bit // 8 :], tiles[: -(bit // 8)])
    for bit in (1, 2, 4):
        tiles = jnp.where((amount & bit) > 0, pltpu.roll(tiles, 8 - bit, 1), tiles)
    inner = lax.broadcasted_iota(jnp.int32, (1, 8, CUT), 1)
    return jnp.where(inner < 8 - (amount & 7), tiles[:-1], tiles[1:]).reshape(count, CUT)


def exchange(
    count,
    old_bounds, new_bounds, failed, states, tokens, cot,
    new_states, act,
    w_in, m_in, ext, e_head, e_tail,
    tok, tok_t, cots, ws, wk_wide, wk, w_mine, w_back, w_arr, m_back, m_arr, r_mine, r_back, r_arr, rims,
    g_all, a_all, g_opp, g_opp_in, g_side, g_side_in, a_opp, a_opp_in, a_side, a_side_in, a_fin, out, g_pad, w_pad, r_pad,
    send, recv, local, tok_send, tok_recv, x_send, x_recv, mate_send, mate_recv, dp_send, dp_recv, misc_send, misc_recv, misc_local,
):
    dp, member = lax.axis_index("dp"), lax.axis_index("fsdp")
    groups, members = lax.axis_size("dp"), lax.axis_size("fsdp")
    y, z = member // SIDE, lax.rem(member, SIDE)
    x, core = dp // 2, lax.rem(dp, 2)
    x_to = [{"dp": lax.rem(x + r, SIDE) * 2 + core} for r in range(SIDE)]
    y_to = [{"fsdp": lax.rem(y + r, SIDE) * SIDE + z} for r in range(SIDE)]
    z_to = [{"fsdp": y * SIDE + lax.rem(z + r, SIDE)} for r in range(SIDE)]
    next_group = lax.rem(dp + 1, groups)
    following, preceding = {"dp": next_group}, {"dp": lax.rem(dp + groups - 1, groups)}
    mate = {"dp": dp + 1 - 2 * core}
    f_up, f_down = {"fsdp": lax.rem(member + 1, members)}, {"fsdp": lax.rem(member + members - 1, members)}

    barrier = pltpu.get_barrier_semaphore()
    peers = [x_to[1], x_to[3]] + y_to[1:] + [z_to[1], z_to[3], following, preceding, mate, f_up, f_down]
    for peer in peers:
        pl.semaphore_signal(barrier, inc=1, device_id=peer, device_id_type=MESH)

    def remote(src, dst, ssem, rsem, peer):
        return pltpu.make_async_remote_copy(
            src_ref=src, dst_ref=dst, send_sem=ssem, recv_sem=rsem, device_id=peer, device_id_type=MESH
        )

    def columns(c):
        return pl.ds(pl.multiple_of(c * CUT, CUT), CUT)

    share = ROWS // 8
    even = lax.rem(x, 2)

    def rows_at(pair, part):
        begin = (pair * 2 + core) * (2 * share)
        if part is None:
            return pl.ds(pl.multiple_of(begin, 2 * share), 2 * share)
        return pl.ds(pl.multiple_of(begin + part * share, share), share)

    def parts(owner):
        span = SIDE * ROWS
        whole = span * SIDE
        begin = pl.multiple_of(owner * span, span)
        before = pl.multiple_of(lax.rem(owner * span + whole - LANE, whole), LANE)
        after = pl.multiple_of(lax.rem(owner * span + span, whole), LANE)
        return (
            (pl.ds(begin, span), pl.ds(LANE, span)),
            (pl.ds(before, LANE), pl.ds(0, LANE)),
            (pl.ds(after, LANE), pl.ds(LANE + span, LANE)),
        )

    def tok_copy(r, k):
        source, target = parts(lax.rem(y + r, SIDE))[k]
        return remote(
            tokens.at[rows_at(even, None), source], tok.at[SIDE - r, rows_at(even, None), target], tok_send.at[r, k], tok_recv.at[r, k], y_to[r]
        )

    def x_copy(k, part):
        rows = rows_at(even, part)
        return remote(
            tok.at[k, rows], tok.at[k, rows], x_send.at[k, part], x_recv.at[k, part], x_to[1 if part == 0 else 3]
        )

    def mate_copy(k, near):
        rows = rows_at(even if near == 0 else 1 - even, None)
        return remote(tok.at[k, rows], tok.at[k, rows], mate_send.at[k, near], mate_recv.at[k, near], mate)

    def w_copy(c):
        return remote(w_back.at[c], w_arr.at[c], dp_send.at[0, c], dp_recv.at[0, c], following)

    def m_copy(c):
        return remote(m_back.at[c], m_arr.at[c], dp_send.at[1, c], dp_recv.at[1, c], following)

    def rim_copy(k):
        if k == 0:
            return remote(r_back, r_arr, misc_send.at[0], misc_recv.at[0], following)
        if k == 1:
            return remote(r_mine.at[0], rims.at[0], misc_send.at[1], misc_recv.at[1], f_down)
        return remote(r_mine.at[1], rims.at[1], misc_send.at[2], misc_recv.at[2], f_up)

    def copy(kind, c):
        src, dst, peer = {
            0: (lambda: (ws.at[c, 0], ws.at[c, 3], z_to[1])),
            1: (lambda: (ws.at[c, 0], ws.at[c, 1], z_to[3])),
            2: (lambda: (ws.at[c, 3, :W_HALF], ws.at[c, 2, :W_HALF], z_to[1])),
            3: (lambda: (ws.at[c, 1, W_HALF:], ws.at[c, 2, W_HALF:], z_to[3])),
            4: (lambda: (cot.at[:, columns(c)], cots.at[c, 3], y_to[1])),
            5: (lambda: (cot.at[:, columns(c)], cots.at[c, 1], y_to[3])),
            6: (lambda: (cots.at[c, 3, :A_HALF], cots.at[c, 2, :A_HALF], y_to[1])),
            7: (lambda: (cots.at[c, 1, A_HALF:], cots.at[c, 2, A_HALF:], y_to[3])),
            8: (lambda: (g_opp.at[c, :G_HALF], g_opp_in.at[c, :G_HALF], z_to[1])),
            9: (lambda: (g_opp.at[c, G_HALF:], g_opp_in.at[c, G_HALF:], z_to[3])),
            10: (lambda: (g_side.at[c, 0], g_side_in.at[c, 0], z_to[1])),
            11: (lambda: (g_side.at[c, 1], g_side_in.at[c, 1], z_to[3])),
            12: (lambda: (a_opp.at[c, :A_HALF], a_opp_in.at[c, :A_HALF], y_to[1])),
            13: (lambda: (a_opp.at[c, A_HALF:], a_opp_in.at[c, A_HALF:], y_to[3])),
            14: (lambda: (a_side.at[c, 0], a_side_in.at[c, 0], y_to[1])),
            15: (lambda: (a_side.at[c, 1], a_side_in.at[c, 1], y_to[3])),
        }[kind]()
        return remote(src, dst, send.at[kind, c], recv.at[kind, c], peer)

    def here(k, c):
        src, dst = {
            0: (lambda: (cot.at[:, columns(c)], cots.at[c, 0])),
            1: (lambda: (states.at[0, :, :, columns(c)], w_in.at[lax.rem(c, 3), :, MOVE : MOVE + OLD])),
            2: (lambda: (states.at[1:3, 1, :, columns(c)], m_in.at[lax.rem(c, 2)])),
            3: (lambda: (states.at[:, 0, :, columns(c)], ext.at[lax.rem(c, 3), :, MOVE : MOVE + OLD])),
            4: (lambda: (a_fin.at[c], act.at[:, columns(c)])),
            5: (lambda: (out.at[lax.rem(c, 3)], new_states.at[:, :, columns(c)])),
        }[k]()
        return pltpu.make_async_copy(src, dst, local.at[k, c])

    def mine(k):
        if k < 3:
            source, target = parts(y)[k]
            src, dst = tokens.at[:, source], tok.at[0, :, target]
        elif k == 3:
            src, dst = states.at[:, :, :MOVE], e_head
        else:
            src, dst = states.at[:, :, OLD - 3 * MOVE :], e_tail.at[:, :, : 3 * MOVE]
        return pltpu.make_async_copy(src, dst, misc_local.at[k])

    lost_group = failed[member]
    old_start = old_bounds[dp, member]
    old_len = old_bounds[dp, member + 1] - old_start
    new_start = new_bounds[dp, member]
    new_len = new_bounds[dp, member + 1] - new_start
    back_start = old_bounds[next_group, member]
    back_len = old_bounds[next_group, member + 1] - back_start
    mean_start = ROWS * member
    lost_use = old_len * (lost_group == dp).astype(jnp.int32)
    own_use = old_len - lost_use
    back_use = back_len * (lost_group == next_group).astype(jnp.int32)

    def window(ref, start, usable):
        shift = start - mean_start + NEAR
        place = rows_of(OLD) - shift
        return jnp.where((place >= 0) & (place < usable), rows_from(ref, MOVE - shift, OLD, (16, 8)), 0.0).astype(BF)

    def windows(c):
        slot = lax.rem(c, 3)
        here(1, c).wait()
        w_back[c] = window(w_in.at[slot, 1], back_start, back_use)
        w_copy(c).start()
        w_mine[c] = window(w_in.at[slot, 0], old_start, own_use)

        @pl.when(c + 3 < count)
        def _():
            here(1, c + 3).start()

    def rim_rows():
        mine(3).wait()
        mine(4).wait()
        row = rows_of(MOVE)

        @pl.loop(0, count)
        def _(c):
            for number, (length, usable, rim) in enumerate(((old_len, own_use, r_mine), (back_len, back_use, r_back))):
                some = row < usable
                for state in range(3):
                    head = e_head[state, number, :, columns(c)]
                    tail = rows_from(e_tail.at[state, number, :, columns(c)], length - SHORT, MOVE, (32, 16, 8))
                    rim[0, c, state] = jnp.where(some, head, 0.0).astype(BF)
                    rim[1, c, state] = jnp.where(some, tail, 0.0).astype(BF)

    def moments(c):
        here(2, c).wait()
        m_back[c] = m_in[lax.rem(c, 2)].astype(BF)
        m_copy(c).start()

        @pl.when(c + 2 < count)
        def _():
            here(2, c + 2).start()

    def gather(c):
        copy(4, c).start()
        copy(5, c).start()
        w_copy(c).wait_recv()
        ws[c, 0] = w_mine[c] + w_arr[c]
        copy(0, c).start()
        copy(1, c).start()

    def hand_on(c):
        for kind in (0, 1, 4, 5):
            copy(kind, c).wait_recv()
            copy(kind + 2, c).start()

    def multiply(c):
        slot = lax.rem(c, RING)
        here(0, c).wait()
        copy(6, c).wait_recv()
        copy(7, c).wait_recv()

        @pl.loop(0, TALL // OLD)
        def _(i):
            rows = pl.ds(pl.multiple_of(i * OLD, 16), OLD)
            taken = pl.ds(pl.multiple_of(i * OLD + SKIP, 16), OLD)
            g_all[slot, rows] = jnp.dot(
                tok_t[taken], cots[c].reshape(SIDE * ROWS, CUT), preferred_element_type=F32
            )

        far = pl.ds(pl.multiple_of(lax.rem(z + 2, SIDE) * ROWS + NEAR, NEAR), NEW)
        g_opp[c] = g_all[slot, far].astype(BF)
        copy(8, c).start()
        copy(9, c).start()
        copy(2, c).wait_recv()
        copy(3, c).wait_recv()
        for p in range(SIDE):
            source = lax.rem(p - z + SIDE, SIDE)
            at = LANE - NEAR + ROWS * p
            piece = ws[c, source].astype(F32)
            if p == 0:
                wk_wide[at : at + MOVE] = piece[:MOVE]
            else:
                wk_wide[at : at + MOVE] = wk_wide[at : at + MOVE] + piece[:MOVE]
            wk_wide[at + MOVE : at + OLD] = piece[MOVE:]
        wk[...] = wk_wide[...].astype(BF)

        @pl.loop(0, SIDE)
        def _(r):
            a_all[slot, r] = jnp.dot(tok[r], wk[...], preferred_element_type=F32)

        a_opp[c] = a_all[slot, 2].astype(BF)
        copy(12, c).start()
        copy(13, c).start()

    def add_on(c):
        slot = lax.rem(c, RING)
        copy(8, c).wait_recv()
        copy(9, c).wait_recv()
        up = pl.multiple_of(lax.rem(z + 1, SIDE) * ROWS + NEAR, NEAR)
        down = pl.multiple_of(lax.rem(z + 3, SIDE) * ROWS + NEAR, NEAR)
        g_side[c, 0, :G_HALF] = (g_all[slot, pl.ds(up, G_HALF)] + g_opp_in[c, :G_HALF].astype(F32)).astype(BF)
        g_side[c, 0, G_HALF:] = g_all[slot, pl.ds(up + G_HALF, NEW - G_HALF)].astype(BF)
        g_side[c, 1, :G_HALF] = g_all[slot, pl.ds(down, G_HALF)].astype(BF)
        g_side[c, 1, G_HALF:] = (
            g_all[slot, pl.ds(down + G_HALF, NEW - G_HALF)] + g_opp_in[c, G_HALF:].astype(F32)
        ).astype(BF)
        copy(10, c).start()
        copy(11, c).start()
        copy(12, c).wait_recv()
        copy(13, c).wait_recv()
        a_side[c, 0, :A_HALF] = (a_all[slot, 1, :A_HALF] + a_opp_in[c, :A_HALF].astype(F32)).astype(BF)
        a_side[c, 0, A_HALF:] = a_all[slot, 1, A_HALF:].astype(BF)
        a_side[c, 1, :A_HALF] = a_all[slot, 3, :A_HALF].astype(BF)
        a_side[c, 1, A_HALF:] = (a_all[slot, 3, A_HALF:] + a_opp_in[c, A_HALF:].astype(F32)).astype(BF)
        copy(14, c).start()
        copy(15, c).start()

    def finish(c):
        slot = lax.rem(c, RING)
        at = lax.rem(c, 3)
        row = rows_of(OLD)
        here(3, c).wait()
        m_copy(c).wait_recv()
        w_pad[:OLD] = w_arr[c].astype(F32)
        moved = []
        for state in range(3):
            if state == 0:
                back = rows_from(w_pad, old_start - mean_start + NEAR, OLD, (16, 8))
            else:
                back = m_arr[c, state - 1].astype(F32)
            r_pad[2 * MOVE : 3 * MOVE] = rims[0, c, state].astype(F32)
            late = rows_from(r_pad, 2 * MOVE - (old_len - SHORT), 3 * MOVE, (32, 16, 8))
            value = jnp.where(row < lost_use, back, ext[at, state, MOVE : MOVE + OLD])
            value = jnp.where(row < old_len, value, 0.0)
            ext[at, state, :MOVE] = rims[1, c, state].astype(F32)
            ext[at, state, MOVE : MOVE + SHORT] = value[:SHORT]
            ext[at, state, MOVE + SHORT : MOVE + OLD] = value[SHORT:] + late[: OLD - SHORT]
            ext[at, state, MOVE + OLD : MOVE + OLD + MOVE] = late[OLD - SHORT :]
            moved.append(rows_from(ext.at[at, state], MOVE + new_start - old_start, NEW, (32, 16, 8)))
        copy(14, c).wait_recv()
        copy(15, c).wait_recv()
        a_fin[c] = (a_all[slot, 0] + a_side_in[c, 0].astype(F32) + a_side_in[c, 1].astype(F32)).astype(BF)
        here(4, c).start()
        copy(10, c).wait_recv()
        copy(11, c).wait_recv()
        rows = pl.ds(pl.multiple_of(z * ROWS + NEAR, NEAR), NEW)
        g_pad[:NEW] = g_all[slot, rows] + g_side_in[c, 0].astype(F32) + g_side_in[c, 1].astype(F32)
        grad = rows_from(g_pad, new_start - mean_start + FAR, NEW, (32, 16, 8))
        weight, one, two = moved
        one = beta_one * one + (1.0 - beta_one) * grad
        two = beta_two * two + (1.0 - beta_two) * grad * grad
        direction = one / correct_one / (jnp.sqrt(two / correct_two) + epsilon) + decay_rate * weight
        inside = rows_of(NEW) < new_len

        @pl.when(c >= 3)
        def _():
            here(5, c - 3).wait()

        out[at, 0] = jnp.where(inside, weight - learn_rate * direction, 0.0)
        out[at, 1] = jnp.where(inside, one, 0.0)
        out[at, 2] = jnp.where(inside, two, 0.0)
        here(5, c).start()

    for c in range(3):
        here(1, c).start()
    for k in range(5):
        mine(k).start()
    for c in range(2):
        here(2, c).start()

    @pl.loop(0, count)
    def _(c):
        here(0, c).start()

    wk_wide[:LANE] = jnp.zeros((LANE, CUT), F32)
    wk_wide[LANE + SIDE * ROWS :] = jnp.zeros((LANE, CUT), F32)
    r_pad[...] = jnp.zeros(r_pad.shape, F32)
    pl.semaphore_wait(barrier, len(peers))
    for r in (1, 3, 2):
        for k in range(3):
            tok_copy(r, k).start()
    first = -PRE

    @pl.loop(0, count + END + PRE)
    def _(step):
        t = step + first

        @pl.when(t + PRE < count)
        def _():
            windows(t + PRE)

        @pl.when((t + AHEAD >= 0) & (t + AHEAD < count))
        def _():
            gather(t + AHEAD)

        @pl.when(t == -AHEAD)
        def _():
            rim_rows()
            rim_copy(0).start()

        @pl.when(t == TOK_ONE)
        def _():
            for r in (1, 3, 2):
                for k in range(3):
                    tok_copy(r, k).wait_recv()
                x_copy(SIDE - r, 0).start()
                x_copy(SIDE - r, 1).start()
                mate_copy(SIDE - r, 0).start()

        @pl.when((t + HAND >= 0) & (t + HAND < count))
        def _():
            hand_on(t + HAND)

        @pl.when((t + MOM >= 0) & (t + MOM < count))
        def _():
            moments(t + MOM)

        @pl.when(t == -1)
        def _():
            rim_copy(0).wait_recv()
            r_mine[...] = r_mine[...] + r_arr[...]
            rim_copy(1).start()
            rim_copy(2).start()

        @pl.when(t == TOK_TWO)
        def _():
            for k in range(3):
                mine(k).wait()
            tok_t[:, :ROWS] = tok[0].T
            for k in (3, 1, 2):
                x_copy(k, 0).wait_recv()
                x_copy(k, 1).wait_recv()
                mate_copy(k, 1).start()

        @pl.when(t == TOK_END)
        def _():
            for k in (3, 1, 2):
                mate_copy(k, 0).wait_recv()
                mate_copy(k, 1).wait_recv()
                tok_t[:, ROWS * k : ROWS * (k + 1)] = tok[k].T

        @pl.when((t >= ADD) & (t < count + ADD))
        def _():
            add_on(t - ADD)

        @pl.when((t >= 0) & (t < count))
        def _():
            multiply(t)

        @pl.when((t >= END - LOAD) & (t < count + END - LOAD))
        def _():
            here(3, t - END + LOAD).start()

        @pl.when(t == END)
        def _():
            rim_copy(1).wait_recv()
            rim_copy(2).wait_recv()

        @pl.when(t >= END)
        def _():
            finish(t - END)

    @pl.loop(0, count)
    def _(c):
        for kind in range(16):
            copy(kind, c).wait_send()
        w_copy(c).wait_send()
        m_copy(c).wait_send()
        here(4, c).wait()

    for c in range(count - 3, count):
        here(5, c).wait()
    for r in (1, 2, 3):
        for k in range(3):
            tok_copy(r, k).wait_send()
        for k in range(2):
            x_copy(r, k).wait_send()
            mate_copy(r, k).wait_send()
    for k in range(3):
        rim_copy(k).wait_send()


def body(old_states, old_bounds, new_bounds, failed, tokens, cotangent):
    width = cotangent.shape[1]
    count = width // CUT
    smem = pl.BlockSpec(memory_space=pltpu.SMEM)
    hbm = pl.BlockSpec(memory_space=pl.ANY)
    shape = jax.ShapeDtypeStruct
    vm = pltpu.VMEM
    dma = pltpu.SemaphoreType.DMA
    new_states, act = pl.pallas_call(
        lambda *refs: exchange(count, *refs),
        in_specs=[smem, smem, smem, hbm, hbm, hbm],
        out_specs=[hbm, hbm],
        out_shape=[shape((3, NEW, width), F32), shape((ROWS, width), BF)],
        scratch_shapes=[
            vm((3, 2, OLD + 2 * MOVE + 8, CUT), F32),
            vm((2, 2, OLD, CUT), F32),
            vm((3, 3, NEW + SPARE, CUT), F32),
            vm((3, 2, MOVE, width), F32),
            vm((3, 2, MOVE + SPARE, width), F32),
            vm((SIDE, ROWS, DEPTH), BF),
            vm((DEPTH, SIDE * ROWS), BF),
            vm((count, SIDE, ROWS, CUT), BF),
            vm((count, SIDE, OLD, CUT), BF),
            vm((DEPTH, CUT), F32),
            vm((DEPTH, CUT), BF),
            vm((count, OLD, CUT), BF),
            vm((count, OLD, CUT), BF),
            vm((count, OLD, CUT), BF),
            vm((count, 2, OLD, CUT), BF),
            vm((count, 2, OLD, CUT), BF),
            vm((2, count, 3, MOVE, CUT), BF),
            vm((2, count, 3, MOVE, CUT), BF),
            vm((2, count, 3, MOVE, CUT), BF),
            vm((2, count, 3, MOVE, CUT), BF),
            vm((RING, TALL, CUT), F32),
            vm((RING, SIDE, ROWS, CUT), F32),
            vm((count, NEW, CUT), BF),
            vm((count, NEW, CUT), BF),
            vm((count, 2, NEW, CUT), BF),
            vm((count, 2, NEW, CUT), BF),
            vm((count, ROWS, CUT), BF),
            vm((count, ROWS, CUT), BF),
            vm((count, 2, ROWS, CUT), BF),
            vm((count, 2, ROWS, CUT), BF),
            vm((count, ROWS, CUT), BF),
            vm((3, 3, NEW, CUT), F32),
            vm((NEW + SPARE, CUT), F32),
            vm((OLD + SPARE, CUT), F32),
            vm((3 * MOVE + SPARE, CUT), F32),
            dma((16, count)),
            dma((16, count)),
            dma((6, count)),
            dma((SIDE, 3)),
            dma((SIDE, 3)),
            dma((SIDE, 2)),
            dma((SIDE, 2)),
            dma((SIDE, 2)),
            dma((SIDE, 2)),
            dma((2, count)),
            dma((2, count)),
            dma((3,)),
            dma((3,)),
            dma((5,)),
        ],
        compiler_params=pltpu.CompilerParams(
            collective_id=0, has_side_effects=True, vmem_limit_bytes=60 * 2**20
        ),
        name="exchange",
    )(old_bounds, new_bounds, failed, old_states, tokens, cotangent)
    return new_states, act


def solution(mesh):
    in_specs = (
        P(None, None, ("dp", "fsdp"), None),
        P(),
        P(),
        P(),
        P("fsdp", None),
        P("fsdp", "dp"),
    )
    out_specs = (P(None, ("dp", "fsdp"), None), P("fsdp", "dp"))
    return jax.shard_map(body, mesh=mesh, in_specs=in_specs, out_specs=out_specs, check_vma=False)
```

```python
import jax
import jax.numpy as jnp
from jax import lax
from jax.experimental import pallas as pl
from jax.experimental.pallas import tpu as pltpu
from jax.sharding import PartitionSpec as P

beta_one = 0.9
beta_two = 0.95
learn_rate = 0.01
decay_rate = 0.1
epsilon = 1e-08
correct_one = 1.0 - 0.9**8
correct_two = 1.0 - 0.95**8

MESH = pl.DeviceIdType.MESH
SIDE = 4
ROWS = 256
NEAR = 8
FAR = 24
MOVE = 16
SHORT = ROWS - 2 * NEAR
OLD = ROWS + 2 * NEAR
NEW = ROWS + 2 * FAR
CUT = 256
SPARE = 64
LANE = 128
DEPTH = SIDE * ROWS + 2 * LANE
SKIP = 96
TALL = 1088
W_HALF = 144
G_HALF = 160
A_HALF = 128
PRE = 7
AHEAD = 5
HAND = 2
MOM = 1
TOK_ONE = -3
TOK_TWO = -1
TOK_END = 0
ADD = 2
END = 4
LOAD = 1
RING = END + 1
BF = jnp.bfloat16
F32 = jnp.float32


def rows_of(count):
    return lax.broadcasted_iota(jnp.int32, (count, CUT), 0)


def rows_from(ref, start, count, coarse):
    tiles = ref[: count + 8 + sum(coarse), :].reshape(count // 8 + 1 + sum(coarse) // 8, 8, CUT)
    amount = jnp.broadcast_to(start, (1, 8, CUT))
    for bit in coarse:
        tiles = jnp.where((amount & bit) > 0, tiles[bit // 8 :], tiles[: -(bit // 8)])
    for bit in (1, 2, 4):
        tiles = jnp.where((amount & bit) > 0, pltpu.roll(tiles, 8 - bit, 1), tiles)
    inner = lax.broadcasted_iota(jnp.int32, (1, 8, CUT), 1)
    return jnp.where(inner < 8 - (amount & 7), tiles[:-1], tiles[1:]).reshape(count, CUT)


def exchange(
    count,
    old_bounds, new_bounds, failed, states, tokens, cot,
    new_states, act,
    w_in, m_in, ext, e_head, e_tail,
    tok, tok_t, cots, ws, wk_wide, wk, w_mine, w_back, w_arr, m_back, m_arr, r_mine, r_back, r_arr, rims,
    g_all, a_all, g_opp, g_opp_in, g_side, g_side_in, a_opp, a_opp_in, a_side, a_side_in, g_pad, w_pad, r_pad,
    send, recv, local, tok_send, tok_recv, x_send, x_recv, mate_send, mate_recv, dp_send, dp_recv, misc_send, misc_recv, misc_local,
):
    dp, member = lax.axis_index("dp"), lax.axis_index("fsdp")
    groups, members = lax.axis_size("dp"), lax.axis_size("fsdp")
    y, z = member // SIDE, lax.rem(member, SIDE)
    x, core = dp // 2, lax.rem(dp, 2)
    x_to = [{"dp": lax.rem(x + r, SIDE) * 2 + core} for r in range(SIDE)]
    y_to = [{"fsdp": lax.rem(y + r, SIDE) * SIDE + z} for r in range(SIDE)]
    z_to = [{"fsdp": y * SIDE + lax.rem(z + r, SIDE)} for r in range(SIDE)]
    next_group = lax.rem(dp + 1, groups)
    following, preceding = {"dp": next_group}, {"dp": lax.rem(dp + groups - 1, groups)}
    mate = {"dp": dp + 1 - 2 * core}
    f_up, f_down = {"fsdp": lax.rem(member + 1, members)}, {"fsdp": lax.rem(member + members - 1, members)}

    barrier = pltpu.get_barrier_semaphore()
    peers = [x_to[1], x_to[3]] + y_to[1:] + [z_to[1], z_to[3], following, preceding, mate, f_up, f_down]
    for peer in peers:
        pl.semaphore_signal(barrier, inc=1, device_id=peer, device_id_type=MESH)

    def remote(src, dst, ssem, rsem, peer):
        return pltpu.make_async_remote_copy(
            src_ref=src, dst_ref=dst, send_sem=ssem, recv_sem=rsem, device_id=peer, device_id_type=MESH
        )

    def columns(c):
        return pl.ds(pl.multiple_of(c * CUT, CUT), CUT)

    share = ROWS // 8
    even = lax.rem(x, 2)

    def rows_at(pair, part):
        begin = (pair * 2 + core) * (2 * share)
        if part is None:
            return pl.ds(pl.multiple_of(begin, 2 * share), 2 * share)
        return pl.ds(pl.multiple_of(begin + part * share, share), share)

    def parts(owner):
        span = SIDE * ROWS
        whole = span * SIDE
        begin = pl.multiple_of(owner * span, span)
        before = pl.multiple_of(lax.rem(owner * span + whole - LANE, whole), LANE)
        after = pl.multiple_of(lax.rem(owner * span + span, whole), LANE)
        return (
            (pl.ds(begin, span), pl.ds(LANE, span)),
            (pl.ds(before, LANE), pl.ds(0, LANE)),
            (pl.ds(after, LANE), pl.ds(LANE + span, LANE)),
        )

    def tok_copy(r, k):
        source, target = parts(lax.rem(y + r, SIDE))[k]
        return remote(
            tokens.at[rows_at(even, None), source], tok.at[SIDE - r, rows_at(even, None), target], tok_send.at[r, k], tok_recv.at[r, k], y_to[r]
        )

    def x_copy(k, part):
        rows = rows_at(even, part)
        return remote(
            tok.at[k, rows], tok.at[k, rows], x_send.at[k, part], x_recv.at[k, part], x_to[1 if part == 0 else 3]
        )

    def mate_copy(k, near):
        rows = rows_at(even if near == 0 else 1 - even, None)
        return remote(tok.at[k, rows], tok.at[k, rows], mate_send.at[k, near], mate_recv.at[k, near], mate)

    def w_copy(c):
        return remote(w_back.at[c], w_arr.at[c], dp_send.at[0, c], dp_recv.at[0, c], following)

    def m_copy(c):
        return remote(m_back.at[lax.rem(c, 4)], m_arr.at[c], dp_send.at[1, c], dp_recv.at[1, c], following)

    def rim_copy(k):
        if k == 0:
            return remote(r_back, r_arr, misc_send.at[0], misc_recv.at[0], following)
        if k == 1:
            return remote(r_mine.at[0], rims.at[0], misc_send.at[1], misc_recv.at[1], f_down)
        return remote(r_mine.at[1], rims.at[1], misc_send.at[2], misc_recv.at[2], f_up)

    def copy(kind, c):
        src, dst, peer = {
            0: (lambda: (ws.at[c, 0], ws.at[c, 3], z_to[1])),
            1: (lambda: (ws.at[c, 0], ws.at[c, 1], z_to[3])),
            2: (lambda: (ws.at[c, 3, :W_HALF], ws.at[c, 2, :W_HALF], z_to[1])),
            3: (lambda: (ws.at[c, 1, W_HALF:], ws.at[c, 2, W_HALF:], z_to[3])),
            4: (lambda: (cot.at[:, columns(c)], cots.at[c, 3], y_to[1])),
            5: (lambda: (cot.at[:, columns(c)], cots.at[c, 1], y_to[3])),
            6: (lambda: (cots.at[c, 3, :A_HALF], cots.at[c, 2, :A_HALF], y_to[1])),
            7: (lambda: (cots.at[c, 1, A_HALF:], cots.at[c, 2, A_HALF:], y_to[3])),
            8: (lambda: (g_opp.at[c, :G_HALF], g_opp_in.at[c, :G_HALF], z_to[1])),
            9: (lambda: (g_opp.at[c, G_HALF:], g_opp_in.at[c, G_HALF:], z_to[3])),
            10: (lambda: (g_side.at[c, 0], g_side_in.at[c, 0], z_to[1])),
            11: (lambda: (g_side.at[c, 1], g_side_in.at[c, 1], z_to[3])),
            12: (lambda: (a_opp.at[c, :A_HALF], a_opp_in.at[c, :A_HALF], y_to[1])),
            13: (lambda: (a_opp.at[c, A_HALF:], a_opp_in.at[c, A_HALF:], y_to[3])),
            14: (lambda: (a_side.at[c, 0], a_side_in.at[c, 0], y_to[1])),
            15: (lambda: (a_side.at[c, 1], a_side_in.at[c, 1], y_to[3])),
        }[kind]()
        return remote(src, dst, send.at[kind, c], recv.at[kind, c], peer)

    def here(k, c):
        src, dst = {
            0: (lambda: (cot.at[:, columns(c)], cots.at[c, 0])),
            1: (lambda: (states.at[0, :, :, columns(c)], w_in.at[lax.rem(c, 3), :, MOVE : MOVE + OLD])),
            2: (lambda: (states.at[1:3, 1, :, columns(c)], m_in.at[lax.rem(c, 2)])),
            3: (lambda: (states.at[:, 0, :, columns(c)], ext.at[lax.rem(c, 2), :, MOVE : MOVE + OLD])),
        }[k]()
        return pltpu.make_async_copy(src, dst, local.at[k, c])

    def mine(k):
        if k < 3:
            source, target = parts(y)[k]
            src, dst = tokens.at[:, source], tok.at[0, :, target]
        elif k == 3:
            src, dst = states.at[:, :, :MOVE], e_head
        else:
            src, dst = states.at[:, :, OLD - 3 * MOVE :], e_tail.at[:, :, : 3 * MOVE]
        return pltpu.make_async_copy(src, dst, misc_local.at[k])

    lost_group = failed[member]
    old_start = old_bounds[dp, member]
    old_len = old_bounds[dp, member + 1] - old_start
    new_start = new_bounds[dp, member]
    new_len = new_bounds[dp, member + 1] - new_start
    back_start = old_bounds[next_group, member]
    back_len = old_bounds[next_group, member + 1] - back_start
    mean_start = ROWS * member
    lost_use = old_len * (lost_group == dp).astype(jnp.int32)
    own_use = old_len - lost_use
    back_use = back_len * (lost_group == next_group).astype(jnp.int32)

    def window(ref, start, usable):
        shift = start - mean_start + NEAR
        place = rows_of(OLD) - shift
        return jnp.where((place >= 0) & (place < usable), rows_from(ref, MOVE - shift, OLD, (16, 8)), 0.0).astype(BF)

    def back_window(c):
        here(1, c).wait()
        w_back[c] = window(w_in.at[lax.rem(c, 3), 1], back_start, back_use)

    def windows(c):
        slot = lax.rem(c, 3)

        @pl.when(c > 0)
        def _():
            back_window(c)
            w_copy(c).start()

        w_mine[lax.rem(c, 4)] = window(w_in.at[slot, 0], old_start, own_use)

        @pl.when(c + 3 < count)
        def _():
            here(1, c + 3).start()

    def rim_rows():
        mine(3).wait()
        mine(4).wait()
        row = rows_of(MOVE)

        @pl.loop(0, count)
        def _(c):
            for number, (length, usable, rim) in enumerate(((old_len, own_use, r_mine), (back_len, back_use, r_back))):
                some = row < usable
                for state in range(3):
                    head = e_head[state, number, :, columns(c)]
                    tail = rows_from(e_tail.at[state, number, :, columns(c)], length - SHORT, MOVE, (32, 16, 8))
                    rim[0, c, state] = jnp.where(some, head, 0.0).astype(BF)
                    rim[1, c, state] = jnp.where(some, tail, 0.0).astype(BF)

    def moments(c):
        here(2, c).wait()

        @pl.when(c >= 4)
        def _():
            m_copy(c - 4).wait_send()

        m_back[lax.rem(c, 4)] = m_in[lax.rem(c, 2)].astype(BF)
        m_copy(c).start()

        @pl.when(c + 2 < count)
        def _():
            here(2, c + 2).start()

    def gather(c):
        copy(4, c).start()
        copy(5, c).start()
        w_copy(c).wait_recv()
        ws[c, 0] = w_mine[lax.rem(c, 4)] + w_arr[c]
        copy(0, c).start()
        copy(1, c).start()

    def hand_on(c):
        for kind in (0, 1, 4, 5):
            copy(kind, c).wait_recv()
            copy(kind + 2, c).start()

    def multiply(c):
        slot = lax.rem(c, RING)
        here(0, c).wait()
        copy(6, c).wait_recv()
        copy(7, c).wait_recv()

        @pl.loop(0, TALL // OLD)
        def _(i):
            rows = pl.ds(pl.multiple_of(i * OLD, 16), OLD)
            taken = pl.ds(pl.multiple_of(i * OLD + SKIP, 16), OLD)
            g_all[slot, rows] = jnp.dot(
                tok_t[taken], cots[c].reshape(SIDE * ROWS, CUT), preferred_element_type=F32
            )

        far = pl.ds(pl.multiple_of(lax.rem(z + 2, SIDE) * ROWS + NEAR, NEAR), NEW)
        g_opp[c] = g_all[slot, far].astype(BF)
        copy(8, c).start()
        copy(9, c).start()
        copy(2, c).wait_recv()
        copy(3, c).wait_recv()
        for p in range(SIDE):
            source = lax.rem(p - z + SIDE, SIDE)
            at = LANE - NEAR + ROWS * p
            piece = ws[c, source].astype(F32)
            if p == 0:
                wk_wide[at : at + MOVE] = piece[:MOVE]
            else:
                wk_wide[at : at + MOVE] = wk_wide[at : at + MOVE] + piece[:MOVE]
            wk_wide[at + MOVE : at + OLD] = piece[MOVE:]
        wk[...] = wk_wide[...].astype(BF)

        a_opp[c] = jnp.dot(tok[2], wk[...], preferred_element_type=F32).astype(BF)
        copy(12, c).start()
        copy(13, c).start()

        @pl.loop(0, 3)
        def _(k):
            a_all[slot, k] = jnp.dot(tok[k + k // 2], wk[...], preferred_element_type=F32)

    def add_on(c):
        slot = lax.rem(c, RING)
        copy(8, c).wait_recv()
        copy(9, c).wait_recv()
        up = pl.multiple_of(lax.rem(z + 1, SIDE) * ROWS + NEAR, NEAR)
        down = pl.multiple_of(lax.rem(z + 3, SIDE) * ROWS + NEAR, NEAR)
        g_side[c, 0, :G_HALF] = (g_all[slot, pl.ds(up, G_HALF)] + g_opp_in[c, :G_HALF].astype(F32)).astype(BF)
        g_side[c, 0, G_HALF:] = g_all[slot, pl.ds(up + G_HALF, NEW - G_HALF)].astype(BF)
        g_side[c, 1, :G_HALF] = g_all[slot, pl.ds(down, G_HALF)].astype(BF)
        g_side[c, 1, G_HALF:] = (
            g_all[slot, pl.ds(down + G_HALF, NEW - G_HALF)] + g_opp_in[c, G_HALF:].astype(F32)
        ).astype(BF)
        copy(10, c).start()
        copy(11, c).start()
        copy(12, c).wait_recv()
        copy(13, c).wait_recv()
        a_side[c, 0, :A_HALF] = (a_all[slot, 1, :A_HALF] + a_opp_in[c, :A_HALF].astype(F32)).astype(BF)
        a_side[c, 0, A_HALF:] = a_all[slot, 1, A_HALF:].astype(BF)
        a_side[c, 1, :A_HALF] = a_all[slot, 2, :A_HALF].astype(BF)
        a_side[c, 1, A_HALF:] = (a_all[slot, 2, A_HALF:] + a_opp_in[c, A_HALF:].astype(F32)).astype(BF)
        copy(14, c).start()
        copy(15, c).start()

    def finish(c):
        slot = lax.rem(c, RING)
        at = lax.rem(c, 2)
        row = rows_of(OLD)
        here(3, c).wait()
        m_copy(c).wait_recv()
        w_pad[:OLD] = w_arr[c].astype(F32)
        moved = []
        for state in range(3):
            if state == 0:
                back = rows_from(w_pad, old_start - mean_start + NEAR, OLD, (16, 8))
            else:
                back = m_arr[c, state - 1].astype(F32)
            r_pad[2 * MOVE : 3 * MOVE] = rims[0, c, state].astype(F32)
            late = rows_from(r_pad, 2 * MOVE - (old_len - SHORT), 3 * MOVE, (32, 16, 8))
            value = jnp.where(row < lost_use, back, ext[at, state, MOVE : MOVE + OLD])
            value = jnp.where(row < old_len, value, 0.0)
            ext[at, state, :MOVE] = rims[1, c, state].astype(F32)
            ext[at, state, MOVE : MOVE + SHORT] = value[:SHORT]
            ext[at, state, MOVE + SHORT : MOVE + OLD] = value[SHORT:] + late[: OLD - SHORT]
            ext[at, state, MOVE + OLD : MOVE + OLD + MOVE] = late[OLD - SHORT :]
            moved.append(rows_from(ext.at[at, state], MOVE + new_start - old_start, NEW, (32, 16, 8)))
        copy(14, c).wait_recv()
        copy(15, c).wait_recv()
        act[:, columns(c)] = (a_all[slot, 0] + a_side_in[c, 0].astype(F32) + a_side_in[c, 1].astype(F32)).astype(BF)
        copy(10, c).wait_recv()
        copy(11, c).wait_recv()
        rows = pl.ds(pl.multiple_of(z * ROWS + NEAR, NEAR), NEW)
        g_pad[:NEW] = g_all[slot, rows] + g_side_in[c, 0].astype(F32) + g_side_in[c, 1].astype(F32)
        grad = rows_from(g_pad, new_start - mean_start + FAR, NEW, (32, 16, 8))
        weight, one, two = moved
        one = beta_one * one + (1.0 - beta_one) * grad
        two = beta_two * two + (1.0 - beta_two) * grad * grad
        direction = one / correct_one / (jnp.sqrt(two / correct_two) + epsilon) + decay_rate * weight
        inside = rows_of(NEW) < new_len

        new_states[0, :, columns(c)] = jnp.where(inside, weight - learn_rate * direction, 0.0)
        new_states[1, :, columns(c)] = jnp.where(inside, one, 0.0)
        new_states[2, :, columns(c)] = jnp.where(inside, two, 0.0)

    for c in range(3):
        here(1, c).start()
    for k in range(5):
        mine(k).start()
    for c in range(2):
        here(2, c).start()

    @pl.loop(0, count)
    def _(c):
        here(0, c).start()

    wk_wide[:LANE] = jnp.zeros((LANE, CUT), F32)
    wk_wide[LANE + SIDE * ROWS :] = jnp.zeros((LANE, CUT), F32)
    r_pad[...] = jnp.zeros(r_pad.shape, F32)
    back_window(0)
    pl.semaphore_wait(barrier, len(peers))
    for r in (1, 3, 2):
        for k in range(3):
            tok_copy(r, k).start()
    w_copy(0).start()
    first = -PRE

    @pl.loop(0, count + END + PRE)
    def _(step):
        t = step + first

        @pl.when(t + PRE < count)
        def _():
            windows(t + PRE)

        @pl.when((t + AHEAD >= 0) & (t + AHEAD < count))
        def _():
            gather(t + AHEAD)

        @pl.when(t == -AHEAD)
        def _():
            rim_rows()
            rim_copy(0).start()

        @pl.when(t == TOK_ONE)
        def _():
            for r in (1, 3, 2):
                for k in range(3):
                    tok_copy(r, k).wait_recv()
                x_copy(SIDE - r, 0).start()
                x_copy(SIDE - r, 1).start()
                mate_copy(SIDE - r, 0).start()

        @pl.when((t + HAND >= 0) & (t + HAND < count))
        def _():
            hand_on(t + HAND)

        @pl.when((t + MOM >= 0) & (t + MOM < count))
        def _():
            moments(t + MOM)

        @pl.when(t == -1)
        def _():
            rim_copy(0).wait_recv()
            r_mine[...] = r_mine[...] + r_arr[...]
            rim_copy(1).start()
            rim_copy(2).start()

        @pl.when(t == TOK_TWO)
        def _():
            for k in range(3):
                mine(k).wait()
            tok_t[:, :ROWS] = tok[0].T
            for k in (3, 1, 2):
                x_copy(k, 0).wait_recv()
                x_copy(k, 1).wait_recv()
                mate_copy(k, 1).start()

        @pl.when(t == TOK_END)
        def _():
            for k in (3, 1, 2):
                mate_copy(k, 0).wait_recv()
                mate_copy(k, 1).wait_recv()
                tok_t[:, ROWS * k : ROWS * (k + 1)] = tok[k].T

        @pl.when((t >= ADD) & (t < count + ADD))
        def _():
            add_on(t - ADD)

        @pl.when((t >= 0) & (t < count))
        def _():
            multiply(t)

        @pl.when((t >= END - LOAD) & (t < count + END - LOAD))
        def _():
            here(3, t - END + LOAD).start()

        @pl.when(t == END)
        def _():
            rim_copy(1).wait_recv()
            rim_copy(2).wait_recv()

        @pl.when(t >= END)
        def _():
            finish(t - END)

    @pl.loop(0, count)
    def _(c):
        for kind in range(16):
            copy(kind, c).wait_send()
        w_copy(c).wait_send()

    for c in range(count - 4, count):
        m_copy(c).wait_send()
    for r in (1, 2, 3):
        for k in range(3):
            tok_copy(r, k).wait_send()
        for k in range(2):
            x_copy(r, k).wait_send()
            mate_copy(r, k).wait_send()
    for k in range(3):
        rim_copy(k).wait_send()


def body(old_states, old_bounds, new_bounds, failed, tokens, cotangent):
    width = cotangent.shape[1]
    count = width // CUT
    smem = pl.BlockSpec(memory_space=pltpu.SMEM)
    hbm = pl.BlockSpec(memory_space=pl.ANY)
    shape = jax.ShapeDtypeStruct
    vm = pltpu.VMEM
    dma = pltpu.SemaphoreType.DMA
    new_states, act = pl.pallas_call(
        lambda *refs: exchange(count, *refs),
        in_specs=[smem, smem, smem, hbm, hbm, hbm],
        out_specs=[pl.BlockSpec(memory_space=vm)] * 2,
        out_shape=[vm((3, NEW, width), F32), vm((ROWS, width), BF)],
        scratch_shapes=[
            vm((3, 2, OLD + 2 * MOVE + 8, CUT), F32),
            vm((2, 2, OLD, CUT), F32),
            vm((2, 3, NEW + SPARE, CUT), F32),
            vm((3, 2, MOVE, width), F32),
            vm((3, 2, MOVE + SPARE, width), F32),
            vm((SIDE, ROWS, DEPTH), BF),
            vm((DEPTH, SIDE * ROWS), BF),
            vm((count, SIDE, ROWS, CUT), BF),
            vm((count, SIDE, OLD, CUT), BF),
            vm((DEPTH, CUT), F32),
            vm((DEPTH, CUT), BF),
            vm((4, OLD, CUT), BF),
            vm((count, OLD, CUT), BF),
            vm((count, OLD, CUT), BF),
            vm((4, 2, OLD, CUT), BF),
            vm((count, 2, OLD, CUT), BF),
            vm((2, count, 3, MOVE, CUT), BF),
            vm((2, count, 3, MOVE, CUT), BF),
            vm((2, count, 3, MOVE, CUT), BF),
            vm((2, count, 3, MOVE, CUT), BF),
            vm((RING, TALL, CUT), F32),
            vm((RING, 3, ROWS, CUT), F32),
            vm((count, NEW, CUT), BF),
            vm((count, NEW, CUT), BF),
            vm((count, 2, NEW, CUT), BF),
            vm((count, 2, NEW, CUT), BF),
            vm((count, ROWS, CUT), BF),
            vm((count, ROWS, CUT), BF),
            vm((count, 2, ROWS, CUT), BF),
            vm((count, 2, ROWS, CUT), BF),
            vm((NEW + SPARE, CUT), F32),
            vm((OLD + SPARE, CUT), F32),
            vm((3 * MOVE + SPARE, CUT), F32),
            dma((16, count)),
            dma((16, count)),
            dma((4, count)),
            dma((SIDE, 3)),
            dma((SIDE, 3)),
            dma((SIDE, 2)),
            dma((SIDE, 2)),
            dma((SIDE, 2)),
            dma((SIDE, 2)),
            dma((2, count)),
            dma((2, count)),
            dma((3,)),
            dma((3,)),
            dma((5,)),
        ],
        compiler_params=pltpu.CompilerParams(
            collective_id=0, has_side_effects=True, vmem_limit_bytes=54 * 2**20
        ),
        name="exchange",
    )(old_bounds, new_bounds, failed, old_states, tokens, cotangent)
    return new_states, act


def solution(mesh):
    in_specs = (
        P(None, None, ("dp", "fsdp"), None),
        P(),
        P(),
        P(),
        P("fsdp", None),
        P("fsdp", "dp"),
    )
    out_specs = (P(None, ("dp", "fsdp"), None), P("fsdp", "dp"))
    return jax.shard_map(body, mesh=mesh, in_specs=in_specs, out_specs=out_specs, check_vma=False)
```

```python
import jax
import jax.numpy as jnp
from jax import lax
from jax.experimental import pallas as pl
from jax.experimental.pallas import tpu as pltpu
from jax.sharding import PartitionSpec as P

beta_one = 0.9
beta_two = 0.95
learn_rate = 0.01
decay_rate = 0.1
epsilon = 1e-08
correct_one = 1.0 - 0.9**8
correct_two = 1.0 - 0.95**8

MESH = pl.DeviceIdType.MESH
SIDE = 4
ROWS = 256
NEAR = 8
FAR = 24
MOVE = 16
SHORT = ROWS - 2 * NEAR
OLD = ROWS + 2 * NEAR
NEW = ROWS + 2 * FAR
CUT = 256
SPARE = 64
LANE = 128
DEPTH = SIDE * ROWS + 2 * LANE
SKIP = 96
TALL = 1088
W_HALF = 128
G_HALF = 160
A_HALF = 128
PRE = 7
AHEAD = 5
HAND = 2
MOM = 1
TOK_ONE = -3
TOK_TWO = -1
TOK_END = 0
ADD = 2
END = 4
LOAD = 1
RING = END + 1
BF = jnp.bfloat16
F32 = jnp.float32


def rows_of(count):
    return lax.broadcasted_iota(jnp.int32, (count, CUT), 0)


def rows_from(ref, start, count, coarse):
    tiles = ref[: count + 8 + sum(coarse), :].reshape(count // 8 + 1 + sum(coarse) // 8, 8, CUT)
    amount = jnp.broadcast_to(start, (1, 8, CUT))
    for bit in coarse:
        tiles = jnp.where((amount & bit) > 0, tiles[bit // 8 :], tiles[: -(bit // 8)])
    for bit in (1, 2, 4):
        tiles = jnp.where((amount & bit) > 0, pltpu.roll(tiles, 8 - bit, 1), tiles)
    inner = lax.broadcasted_iota(jnp.int32, (1, 8, CUT), 1)
    return jnp.where(inner < 8 - (amount & 7), tiles[:-1], tiles[1:]).reshape(count, CUT)


def exchange(
    count,
    old_bounds, new_bounds, failed, states, tokens, cot,
    new_states, act,
    w_in, m_in, ext, e_head, e_tail,
    tok, tok_t, cots, ws, wk_wide, wk, w_mine, w_back, w_arr, m_back, m_arr, r_mine, r_back, r_arr, rims,
    g_all, a_all, g_opp, g_opp_in, g_side, g_side_in, a_opp, a_opp_in, a_side, a_side_in, g_pad, w_pad, r_pad,
    send, recv, local, tok_send, tok_recv, x_send, x_recv, mate_send, mate_recv, dp_send, dp_recv, misc_send, misc_recv, misc_local,
):
    dp, member = lax.axis_index("dp"), lax.axis_index("fsdp")
    groups, members = lax.axis_size("dp"), lax.axis_size("fsdp")
    y, z = member // SIDE, lax.rem(member, SIDE)
    x, core = dp // 2, lax.rem(dp, 2)
    x_to = [{"dp": lax.rem(x + r, SIDE) * 2 + core} for r in range(SIDE)]
    y_to = [{"fsdp": lax.rem(y + r, SIDE) * SIDE + z} for r in range(SIDE)]
    z_to = [{"fsdp": y * SIDE + lax.rem(z + r, SIDE)} for r in range(SIDE)]
    next_group = lax.rem(dp + 1, groups)
    following, preceding = {"dp": next_group}, {"dp": lax.rem(dp + groups - 1, groups)}
    mate = {"dp": dp + 1 - 2 * core}
    f_up, f_down = {"fsdp": lax.rem(member + 1, members)}, {"fsdp": lax.rem(member + members - 1, members)}

    barrier = pltpu.get_barrier_semaphore()
    peers = [x_to[1], x_to[3]] + y_to[1:] + [z_to[1], z_to[3], following, preceding, mate, f_up, f_down]
    for peer in peers:
        pl.semaphore_signal(barrier, inc=1, device_id=peer, device_id_type=MESH)

    def remote(src, dst, ssem, rsem, peer):
        return pltpu.make_async_remote_copy(
            src_ref=src, dst_ref=dst, send_sem=ssem, recv_sem=rsem, device_id=peer, device_id_type=MESH
        )

    def columns(c):
        return pl.ds(pl.multiple_of(c * CUT, CUT), CUT)

    share = ROWS // 8
    even = lax.rem(x, 2)

    def rows_at(pair, part):
        begin = (pair * 2 + core) * (2 * share)
        if part is None:
            return pl.ds(pl.multiple_of(begin, 2 * share), 2 * share)
        return pl.ds(pl.multiple_of(begin + part * share, share), share)

    def parts(owner):
        span = SIDE * ROWS
        whole = span * SIDE
        begin = pl.multiple_of(owner * span, span)
        before = pl.multiple_of(lax.rem(owner * span + whole - LANE, whole), LANE)
        after = pl.multiple_of(lax.rem(owner * span + span, whole), LANE)
        return (
            (pl.ds(begin, span), pl.ds(LANE, span)),
            (pl.ds(before, LANE), pl.ds(0, LANE)),
            (pl.ds(after, LANE), pl.ds(LANE + span, LANE)),
        )

    def tok_copy(r, k):
        source, target = parts(lax.rem(y + r, SIDE))[k]
        return remote(
            tokens.at[rows_at(even, None), source], tok.at[SIDE - r, rows_at(even, None), target], tok_send.at[r, k], tok_recv.at[r, k], y_to[r]
        )

    def x_copy(k, part):
        rows = rows_at(even, part)
        return remote(
            tok.at[k, rows], tok.at[k, rows], x_send.at[k, part], x_recv.at[k, part], x_to[1 if part == 0 else 3]
        )

    def mate_copy(k, near):
        rows = rows_at(even if near == 0 else 1 - even, None)
        return remote(tok.at[k, rows], tok.at[k, rows], mate_send.at[k, near], mate_recv.at[k, near], mate)

    def w_copy(c):
        return remote(w_back.at[c], w_arr.at[c], dp_send.at[0, c], dp_recv.at[0, c], following)

    def m_copy(c):
        return remote(m_back.at[lax.rem(c, 4)], m_arr.at[c], dp_send.at[1, c], dp_recv.at[1, c], following)

    def rim_copy(k):
        if k == 0:
            return remote(r_back, r_arr, misc_send.at[0], misc_recv.at[0], following)
        if k == 1:
            return remote(r_mine.at[0], rims.at[0], misc_send.at[1], misc_recv.at[1], f_down)
        return remote(r_mine.at[1], rims.at[1], misc_send.at[2], misc_recv.at[2], f_up)

    def copy(kind, c):
        src, dst, peer = {
            0: (lambda: (ws.at[c, 0], ws.at[c, 3], z_to[1])),
            1: (lambda: (ws.at[c, 0], ws.at[c, 1], z_to[3])),
            2: (lambda: (ws.at[c, 3, :W_HALF], ws.at[c, 2, :W_HALF], z_to[1])),
            3: (lambda: (ws.at[c, 1, W_HALF:], ws.at[c, 2, W_HALF:], z_to[3])),
            4: (lambda: (cot.at[:, columns(c)], cots.at[c, 3], y_to[1])),
            5: (lambda: (cot.at[:, columns(c)], cots.at[c, 1], y_to[3])),
            6: (lambda: (cots.at[c, 3, :A_HALF], cots.at[c, 2, :A_HALF], y_to[1])),
            7: (lambda: (cots.at[c, 1, A_HALF:], cots.at[c, 2, A_HALF:], y_to[3])),
            8: (lambda: (g_opp.at[c, :G_HALF], g_opp_in.at[c, :G_HALF], z_to[1])),
            9: (lambda: (g_opp.at[c, G_HALF:], g_opp_in.at[c, G_HALF:], z_to[3])),
            10: (lambda: (g_side.at[c, 0], g_side_in.at[c, 0], z_to[1])),
            11: (lambda: (g_side.at[c, 1], g_side_in.at[c, 1], z_to[3])),
            12: (lambda: (a_opp.at[c, :A_HALF], a_opp_in.at[c, :A_HALF], y_to[1])),
            13: (lambda: (a_opp.at[c, A_HALF:], a_opp_in.at[c, A_HALF:], y_to[3])),
            14: (lambda: (a_side.at[c, 0], a_side_in.at[c, 0], y_to[1])),
            15: (lambda: (a_side.at[c, 1], a_side_in.at[c, 1], y_to[3])),
        }[kind]()
        return remote(src, dst, send.at[kind, c], recv.at[kind, c], peer)

    def here(k, c):
        src, dst = {
            0: (lambda: (cot.at[:, columns(c)], cots.at[c, 0])),
            1: (lambda: (states.at[0, :, :, columns(c)], w_in.at[lax.rem(c, 3), :, MOVE : MOVE + OLD])),
            2: (lambda: (states.at[1:3, 1, :, columns(c)], m_in.at[lax.rem(c, 2)])),
            3: (lambda: (states.at[:, 0, :, columns(c)], ext.at[lax.rem(c, 2), :, MOVE : MOVE + OLD])),
        }[k]()
        return pltpu.make_async_copy(src, dst, local.at[k, c])

    def mine(k):
        if k < 3:
            source, target = parts(y)[k]
            src, dst = tokens.at[:, source], tok.at[0, :, target]
        elif k == 3:
            src, dst = states.at[:, :, :MOVE], e_head
        else:
            src, dst = states.at[:, :, OLD - 3 * MOVE :], e_tail.at[:, :, : 3 * MOVE]
        return pltpu.make_async_copy(src, dst, misc_local.at[k])

    lost_group = failed[member]
    old_start = old_bounds[dp, member]
    old_len = old_bounds[dp, member + 1] - old_start
    new_start = new_bounds[dp, member]
    new_len = new_bounds[dp, member + 1] - new_start
    back_start = old_bounds[next_group, member]
    back_len = old_bounds[next_group, member + 1] - back_start
    mean_start = ROWS * member
    lost_use = old_len * (lost_group == dp).astype(jnp.int32)
    own_use = old_len - lost_use
    back_use = back_len * (lost_group == next_group).astype(jnp.int32)

    def window(ref, start, usable):
        shift = start - mean_start + NEAR
        place = rows_of(OLD) - shift
        return jnp.where((place >= 0) & (place < usable), rows_from(ref, MOVE - shift, OLD, (16, 8)), 0.0).astype(BF)

    def back_window(c):
        here(1, c).wait()
        w_back[c] = window(w_in.at[lax.rem(c, 3), 1], back_start, back_use)

    def windows(c):
        slot = lax.rem(c, 3)

        @pl.when(c > 0)
        def _():
            back_window(c)
            w_copy(c).start()

        w_mine[lax.rem(c, 4)] = window(w_in.at[slot, 0], old_start, own_use)

        @pl.when(c + 3 < count)
        def _():
            here(1, c + 3).start()

    def rim_rows():
        mine(3).wait()
        mine(4).wait()
        row = rows_of(MOVE)

        @pl.loop(0, count)
        def _(c):
            for number, (length, usable, rim) in enumerate(((old_len, own_use, r_mine), (back_len, back_use, r_back))):
                some = row < usable
                for state in range(3):
                    head = e_head[state, number, :, columns(c)]
                    tail = rows_from(e_tail.at[state, number, :, columns(c)], length - SHORT, MOVE, (32, 16, 8))
                    rim[0, c, state] = jnp.where(some, head, 0.0).astype(BF)
                    rim[1, c, state] = jnp.where(some, tail, 0.0).astype(BF)

    def moments(c):
        here(2, c).wait()

        @pl.when(c >= 4)
        def _():
            m_copy(c - 4).wait_send()

        m_back[lax.rem(c, 4)] = m_in[lax.rem(c, 2)].astype(BF)
        m_copy(c).start()

        @pl.when(c + 2 < count)
        def _():
            here(2, c + 2).start()

    def gather(c):
        copy(4, c).start()
        copy(5, c).start()
        w_copy(c).wait_recv()
        ws[c, 0] = w_mine[lax.rem(c, 4)] + w_arr[c]
        copy(0, c).start()
        copy(1, c).start()

    def hand_on(c):
        for kind in (0, 1, 4, 5):
            copy(kind, c).wait_recv()
            copy(kind + 2, c).start()

    def multiply(c):
        slot = lax.rem(c, RING)
        here(0, c).wait()
        copy(6, c).wait_recv()
        copy(7, c).wait_recv()

        @pl.loop(0, TALL // OLD)
        def _(i):
            rows = pl.ds(pl.multiple_of(i * OLD, 16), OLD)
            taken = pl.ds(pl.multiple_of(i * OLD + SKIP, 16), OLD)
            g_all[slot, rows] = jnp.dot(
                tok_t[taken], cots[c].reshape(SIDE * ROWS, CUT), preferred_element_type=F32
            )

        far = pl.ds(pl.multiple_of(lax.rem(z + 2, SIDE) * ROWS + NEAR, NEAR), NEW)
        g_opp[c] = g_all[slot, far].astype(BF)
        copy(8, c).start()
        copy(9, c).start()
        copy(2, c).wait_recv()
        copy(3, c).wait_recv()
        for p in range(SIDE):
            source = lax.rem(p - z + SIDE, SIDE)
            at = LANE - NEAR + ROWS * p
            piece = ws[c, source].astype(F32)
            if p == 0:
                wk_wide[at : at + MOVE] = piece[:MOVE]
            else:
                wk_wide[at : at + MOVE] = wk_wide[at : at + MOVE] + piece[:MOVE]
            wk_wide[at + MOVE : at + OLD] = piece[MOVE:]
        wk[...] = wk_wide[...].astype(BF)

        a_opp[c] = jnp.dot(tok[2], wk[...], preferred_element_type=F32).astype(BF)
        copy(12, c).start()
        copy(13, c).start()

        @pl.loop(0, 3)
        def _(k):
            a_all[slot, k] = jnp.dot(tok[k + k // 2], wk[...], preferred_element_type=F32)

    def add_on(c):
        slot = lax.rem(c, RING)
        copy(8, c).wait_recv()
        copy(9, c).wait_recv()
        up = pl.multiple_of(lax.rem(z + 1, SIDE) * ROWS + NEAR, NEAR)
        down = pl.multiple_of(lax.rem(z + 3, SIDE) * ROWS + NEAR, NEAR)
        g_side[c, 0, :G_HALF] = (g_all[slot, pl.ds(up, G_HALF)] + g_opp_in[c, :G_HALF].astype(F32)).astype(BF)
        g_side[c, 0, G_HALF:] = g_all[slot, pl.ds(up + G_HALF, NEW - G_HALF)].astype(BF)
        g_side[c, 1, :G_HALF] = g_all[slot, pl.ds(down, G_HALF)].astype(BF)
        g_side[c, 1, G_HALF:] = (
            g_all[slot, pl.ds(down + G_HALF, NEW - G_HALF)] + g_opp_in[c, G_HALF:].astype(F32)
        ).astype(BF)
        copy(10, c).start()
        copy(11, c).start()
        copy(12, c).wait_recv()
        copy(13, c).wait_recv()
        a_side[c, 0, :A_HALF] = (a_all[slot, 1, :A_HALF] + a_opp_in[c, :A_HALF].astype(F32)).astype(BF)
        a_side[c, 0, A_HALF:] = a_all[slot, 1, A_HALF:].astype(BF)
        a_side[c, 1, :A_HALF] = a_all[slot, 2, :A_HALF].astype(BF)
        a_side[c, 1, A_HALF:] = (a_all[slot, 2, A_HALF:] + a_opp_in[c, A_HALF:].astype(F32)).astype(BF)
        copy(14, c).start()
        copy(15, c).start()

    def finish(c):
        slot = lax.rem(c, RING)
        at = lax.rem(c, 2)
        row = rows_of(OLD)
        here(3, c).wait()
        m_copy(c).wait_recv()
        w_pad[:OLD] = w_arr[c].astype(F32)
        moved = []
        for state in range(3):
            if state == 0:
                back = rows_from(w_pad, old_start - mean_start + NEAR, OLD, (16, 8))
            else:
                back = m_arr[c, state - 1].astype(F32)
            r_pad[2 * MOVE : 3 * MOVE] = rims[0, c, state].astype(F32)
            late = rows_from(r_pad, 2 * MOVE - (old_len - SHORT), 3 * MOVE, (32, 16, 8))
            value = jnp.where(row < lost_use, back, ext[at, state, MOVE : MOVE + OLD])
            value = jnp.where(row < old_len, value, 0.0)
            ext[at, state, :MOVE] = rims[1, c, state].astype(F32)
            ext[at, state, MOVE : MOVE + SHORT] = value[:SHORT]
            ext[at, state, MOVE + SHORT : MOVE + OLD] = value[SHORT:] + late[: OLD - SHORT]
            ext[at, state, MOVE + OLD : MOVE + OLD + MOVE] = late[OLD - SHORT :]
            moved.append(rows_from(ext.at[at, state], MOVE + new_start - old_start, NEW, (32, 16, 8)))
        copy(14, c).wait_recv()
        copy(15, c).wait_recv()
        act[:, columns(c)] = (a_all[slot, 0] + a_side_in[c, 0].astype(F32) + a_side_in[c, 1].astype(F32)).astype(BF)
        copy(10, c).wait_recv()
        copy(11, c).wait_recv()
        rows = pl.ds(pl.multiple_of(z * ROWS + NEAR, NEAR), NEW)
        g_pad[:NEW] = g_all[slot, rows] + g_side_in[c, 0].astype(F32) + g_side_in[c, 1].astype(F32)
        grad = rows_from(g_pad, new_start - mean_start + FAR, NEW, (32, 16, 8))
        weight, one, two = moved
        one = beta_one * one + (1.0 - beta_one) * grad
        two = beta_two * two + (1.0 - beta_two) * grad * grad
        direction = one / correct_one / (jnp.sqrt(two / correct_two) + epsilon) + decay_rate * weight
        inside = rows_of(NEW) < new_len

        new_states[0, :, columns(c)] = jnp.where(inside, weight - learn_rate * direction, 0.0)
        new_states[1, :, columns(c)] = jnp.where(inside, one, 0.0)
        new_states[2, :, columns(c)] = jnp.where(inside, two, 0.0)

    for c in range(3):
        here(1, c).start()
    for k in range(5):
        mine(k).start()
    for c in range(2):
        here(2, c).start()

    @pl.loop(0, count)
    def _(c):
        here(0, c).start()

    wk_wide[:LANE] = jnp.zeros((LANE, CUT), F32)
    wk_wide[LANE + SIDE * ROWS :] = jnp.zeros((LANE, CUT), F32)
    r_pad[...] = jnp.zeros(r_pad.shape, F32)
    back_window(0)
    pl.semaphore_wait(barrier, len(peers))
    for r in (1, 3, 2):
        for k in range(3):
            tok_copy(r, k).start()
    w_copy(0).start()
    first = -PRE

    @pl.loop(0, count + END + PRE)
    def _(step):
        t = step + first

        @pl.when(t + PRE < count)
        def _():
            windows(t + PRE)

        @pl.when((t + AHEAD >= 0) & (t + AHEAD < count))
        def _():
            gather(t + AHEAD)

        @pl.when(t == -AHEAD)
        def _():
            rim_rows()
            rim_copy(0).start()

        @pl.when(t == TOK_ONE)
        def _():
            for r in (1, 3, 2):
                for k in range(3):
                    tok_copy(r, k).wait_recv()
                x_copy(SIDE - r, 0).start()
                x_copy(SIDE - r, 1).start()
                mate_copy(SIDE - r, 0).start()

        @pl.when((t + HAND >= 0) & (t + HAND < count))
        def _():
            hand_on(t + HAND)

        @pl.when((t + MOM >= 0) & (t + MOM < count))
        def _():
            moments(t + MOM)

        @pl.when(t == -1)
        def _():
            rim_copy(0).wait_recv()
            r_mine[...] = r_mine[...] + r_arr[...]
            rim_copy(1).start()
            rim_copy(2).start()

        @pl.when(t == TOK_TWO)
        def _():
            for k in range(3):
                mine(k).wait()
            tok_t[:, :ROWS] = tok[0].T
            for k in (3, 1, 2):
                x_copy(k, 0).wait_recv()
                x_copy(k, 1).wait_recv()
                mate_copy(k, 1).start()

        @pl.when(t == TOK_END)
        def _():
            for k in (3, 1, 2):
                mate_copy(k, 0).wait_recv()
                mate_copy(k, 1).wait_recv()
                tok_t[:, ROWS * k : ROWS * (k + 1)] = tok[k].T

        @pl.when((t >= 0) & (t < count))
        def _():
            multiply(t)

        @pl.when((t >= ADD) & (t < count + ADD))
        def _():
            add_on(t - ADD)

        @pl.when((t >= END - LOAD) & (t < count + END - LOAD))
        def _():
            here(3, t - END + LOAD).start()

        @pl.when(t == END)
        def _():
            rim_copy(1).wait_recv()
            rim_copy(2).wait_recv()

        @pl.when(t >= END)
        def _():
            finish(t - END)

    @pl.loop(0, count)
    def _(c):
        for kind in range(16):
            copy(kind, c).wait_send()
        w_copy(c).wait_send()

    for c in range(count - 4, count):
        m_copy(c).wait_send()
    for r in (1, 2, 3):
        for k in range(3):
            tok_copy(r, k).wait_send()
        for k in range(2):
            x_copy(r, k).wait_send()
            mate_copy(r, k).wait_send()
    for k in range(3):
        rim_copy(k).wait_send()


def body(old_states, old_bounds, new_bounds, failed, tokens, cotangent):
    width = cotangent.shape[1]
    count = width // CUT
    smem = pl.BlockSpec(memory_space=pltpu.SMEM)
    hbm = pl.BlockSpec(memory_space=pl.ANY)
    shape = jax.ShapeDtypeStruct
    vm = pltpu.VMEM
    dma = pltpu.SemaphoreType.DMA
    new_states, act = pl.pallas_call(
        lambda *refs: exchange(count, *refs),
        in_specs=[smem, smem, smem, hbm, hbm, hbm],
        out_specs=[pl.BlockSpec(memory_space=vm)] * 2,
        out_shape=[vm((3, NEW, width), F32), vm((ROWS, width), BF)],
        scratch_shapes=[
            vm((3, 2, OLD + 2 * MOVE + 8, CUT), F32),
            vm((2, 2, OLD, CUT), F32),
            vm((2, 3, NEW + SPARE, CUT), F32),
            vm((3, 2, MOVE, width), F32),
            vm((3, 2, MOVE + SPARE, width), F32),
            vm((SIDE, ROWS, DEPTH), BF),
            vm((DEPTH, SIDE * ROWS), BF),
            vm((count, SIDE, ROWS, CUT), BF),
            vm((count, SIDE, OLD, CUT), BF),
            vm((DEPTH, CUT), F32),
            vm((DEPTH, CUT), BF),
            vm((4, OLD, CUT), BF),
            vm((count, OLD, CUT), BF),
            vm((count, OLD, CUT), BF),
            vm((4, 2, OLD, CUT), BF),
            vm((count, 2, OLD, CUT), BF),
            vm((2, count, 3, MOVE, CUT), BF),
            vm((2, count, 3, MOVE, CUT), BF),
            vm((2, count, 3, MOVE, CUT), BF),
            vm((2, count, 3, MOVE, CUT), BF),
            vm((RING, TALL, CUT), F32),
            vm((RING, 3, ROWS, CUT), F32),
            vm((count, NEW, CUT), BF),
            vm((count, NEW, CUT), BF),
            vm((count, 2, NEW, CUT), BF),
            vm((count, 2, NEW, CUT), BF),
            vm((count, ROWS, CUT), BF),
            vm((count, ROWS, CUT), BF),
            vm((count, 2, ROWS, CUT), BF),
            vm((count, 2, ROWS, CUT), BF),
            vm((NEW + SPARE, CUT), F32),
            vm((OLD + SPARE, CUT), F32),
            vm((3 * MOVE + SPARE, CUT), F32),
            dma((16, count)),
            dma((16, count)),
            dma((4, count)),
            dma((SIDE, 3)),
            dma((SIDE, 3)),
            dma((SIDE, 2)),
            dma((SIDE, 2)),
            dma((SIDE, 2)),
            dma((SIDE, 2)),
            dma((2, count)),
            dma((2, count)),
            dma((3,)),
            dma((3,)),
            dma((5,)),
        ],
        compiler_params=pltpu.CompilerParams(
            collective_id=0, has_side_effects=True, vmem_limit_bytes=54 * 2**20
        ),
        name="exchange",
    )(old_bounds, new_bounds, failed, old_states, tokens, cotangent)
    return new_states, act


def solution(mesh):
    in_specs = (
        P(None, None, ("dp", "fsdp"), None),
        P(),
        P(),
        P(),
        P("fsdp", None),
        P("fsdp", "dp"),
    )
    out_specs = (P(None, ("dp", "fsdp"), None), P("fsdp", "dp"))
    return jax.shard_map(body, mesh=mesh, in_specs=in_specs, out_specs=out_specs, check_vma=False)
```

```python
import jax
import jax.numpy as jnp
from jax import lax
from jax.experimental import pallas as pl
from jax.experimental.pallas import tpu as pltpu
from jax.sharding import PartitionSpec as P

beta_one = 0.9
beta_two = 0.95
learn_rate = 0.01
decay_rate = 0.1
epsilon = 1e-08
correct_one = 1.0 - 0.9**8
correct_two = 1.0 - 0.95**8

MESH = pl.DeviceIdType.MESH
SIDE = 4
ROWS = 256
NEAR = 8
FAR = 24
MOVE = 16
SHORT = ROWS - 2 * NEAR
OLD = ROWS + 2 * NEAR
NEW = ROWS + 2 * FAR
CUT = 256
SPARE = 64
LANE = 128
DEPTH = SIDE * ROWS + 2 * LANE
SKIP = 96
TALL = 1088
W_HALF = 128
G_HALF = 160
A_HALF = 128
PRE = 7
AHEAD = 5
HAND = 2
MOM = 1
TOK_ONE = -3
TOK_TWO = -1
TOK_END = 0
ADD = 2
END = 3
LOAD = 1
RING = END + 1
BF = jnp.bfloat16
F32 = jnp.float32


def rows_of(count):
    return lax.broadcasted_iota(jnp.int32, (count, CUT), 0)


def rows_from(ref, start, count, coarse):
    tiles = ref[: count + 8 + sum(coarse), :].reshape(count // 8 + 1 + sum(coarse) // 8, 8, CUT)
    amount = jnp.broadcast_to(start, (1, 8, CUT))
    for bit in coarse:
        tiles = jnp.where((amount & bit) > 0, tiles[bit // 8 :], tiles[: -(bit // 8)])
    for bit in (1, 2, 4):
        tiles = jnp.where((amount & bit) > 0, pltpu.roll(tiles, 8 - bit, 1), tiles)
    inner = lax.broadcasted_iota(jnp.int32, (1, 8, CUT), 1)
    return jnp.where(inner < 8 - (amount & 7), tiles[:-1], tiles[1:]).reshape(count, CUT)


def exchange(
    count,
    old_bounds, new_bounds, failed, states, tokens, cot,
    new_states, act,
    w_in, m_in, ext, e_head, e_tail,
    tok, tok_t, cots, ws, wk_wide, wk, w_mine, w_back, w_arr, m_back, m_arr, r_mine, r_back, r_arr, rims,
    g_all, a_all, g_opp, g_opp_in, g_side, g_side_in, a_opp, a_opp_in, a_side, a_side_in, g_pad, w_pad, r_pad,
    send, recv, local, tok_send, tok_recv, x_send, x_recv, mate_send, mate_recv, dp_send, dp_recv, misc_send, misc_recv, misc_local,
):
    dp, member = lax.axis_index("dp"), lax.axis_index("fsdp")
    groups, members = lax.axis_size("dp"), lax.axis_size("fsdp")
    y, z = member // SIDE, lax.rem(member, SIDE)
    x, core = dp // 2, lax.rem(dp, 2)
    x_to = [{"dp": lax.rem(x + r, SIDE) * 2 + core} for r in range(SIDE)]
    y_to = [{"fsdp": lax.rem(y + r, SIDE) * SIDE + z} for r in range(SIDE)]
    z_to = [{"fsdp": y * SIDE + lax.rem(z + r, SIDE)} for r in range(SIDE)]
    next_group = lax.rem(dp + 1, groups)
    following, preceding = {"dp": next_group}, {"dp": lax.rem(dp + groups - 1, groups)}
    mate = {"dp": dp + 1 - 2 * core}
    f_up, f_down = {"fsdp": lax.rem(member + 1, members)}, {"fsdp": lax.rem(member + members - 1, members)}

    barrier = pltpu.get_barrier_semaphore()
    peers = [x_to[1], x_to[3]] + y_to[1:] + [z_to[1], z_to[3], following, preceding, mate, f_up, f_down]
    for peer in peers:
        pl.semaphore_signal(barrier, inc=1, device_id=peer, device_id_type=MESH)

    def remote(src, dst, ssem, rsem, peer):
        return pltpu.make_async_remote_copy(
            src_ref=src, dst_ref=dst, send_sem=ssem, recv_sem=rsem, device_id=peer, device_id_type=MESH
        )

    def columns(c):
        return pl.ds(pl.multiple_of(c * CUT, CUT), CUT)

    share = ROWS // 8
    even = lax.rem(x, 2)

    def rows_at(pair, part):
        begin = (pair * 2 + core) * (2 * share)
        if part is None:
            return pl.ds(pl.multiple_of(begin, 2 * share), 2 * share)
        return pl.ds(pl.multiple_of(begin + part * share, share), share)

    def parts(owner):
        span = SIDE * ROWS
        whole = span * SIDE
        begin = pl.multiple_of(owner * span, span)
        before = pl.multiple_of(lax.rem(owner * span + whole - LANE, whole), LANE)
        after = pl.multiple_of(lax.rem(owner * span + span, whole), LANE)
        return (
            (pl.ds(begin, span), pl.ds(LANE, span)),
            (pl.ds(before, LANE), pl.ds(0, LANE)),
            (pl.ds(after, LANE), pl.ds(LANE + span, LANE)),
        )

    def tok_copy(r, k):
        source, target = parts(lax.rem(y + r, SIDE))[k]
        return remote(
            tokens.at[rows_at(even, None), source], tok.at[SIDE - r, rows_at(even, None), target], tok_send.at[r, k], tok_recv.at[r, k], y_to[r]
        )

    def x_copy(k, part):
        rows = rows_at(even, part)
        return remote(
            tok.at[k, rows], tok.at[k, rows], x_send.at[k, part], x_recv.at[k, part], x_to[1 if part == 0 else 3]
        )

    def mate_copy(k, near):
        rows = rows_at(even if near == 0 else 1 - even, None)
        return remote(tok.at[k, rows], tok.at[k, rows], mate_send.at[k, near], mate_recv.at[k, near], mate)

    def w_copy(c):
        return remote(w_back.at[c], w_arr.at[c], dp_send.at[0, c], dp_recv.at[0, c], following)

    def m_copy(c):
        return remote(m_back.at[lax.rem(c, 4)], m_arr.at[c], dp_send.at[1, c], dp_recv.at[1, c], following)

    def rim_copy(k):
        if k == 0:
            return remote(r_back, r_arr, misc_send.at[0], misc_recv.at[0], following)
        if k == 1:
            return remote(r_mine.at[0], rims.at[0], misc_send.at[1], misc_recv.at[1], f_down)
        return remote(r_mine.at[1], rims.at[1], misc_send.at[2], misc_recv.at[2], f_up)

    def copy(kind, c):
        src, dst, peer = {
            0: (lambda: (ws.at[c, 0], ws.at[c, 3], z_to[1])),
            1: (lambda: (ws.at[c, 0], ws.at[c, 1], z_to[3])),
            2: (lambda: (ws.at[c, 3, :W_HALF], ws.at[c, 2, :W_HALF], z_to[1])),
            3: (lambda: (ws.at[c, 1, W_HALF:], ws.at[c, 2, W_HALF:], z_to[3])),
            4: (lambda: (cot.at[:, columns(c)], cots.at[c, 3], y_to[1])),
            5: (lambda: (cot.at[:, columns(c)], cots.at[c, 1], y_to[3])),
            6: (lambda: (cots.at[c, 3, :A_HALF], cots.at[c, 2, :A_HALF], y_to[1])),
            7: (lambda: (cots.at[c, 1, A_HALF:], cots.at[c, 2, A_HALF:], y_to[3])),
            8: (lambda: (g_opp.at[c, :G_HALF], g_opp_in.at[c, :G_HALF], z_to[1])),
            9: (lambda: (g_opp.at[c, G_HALF:], g_opp_in.at[c, G_HALF:], z_to[3])),
            10: (lambda: (g_side.at[c, 0], g_side_in.at[c, 0], z_to[1])),
            11: (lambda: (g_side.at[c, 1], g_side_in.at[c, 1], z_to[3])),
            12: (lambda: (a_opp.at[c, :A_HALF], a_opp_in.at[c, :A_HALF], y_to[1])),
            13: (lambda: (a_opp.at[c, A_HALF:], a_opp_in.at[c, A_HALF:], y_to[3])),
            14: (lambda: (a_side.at[c, 0], a_side_in.at[c, 0], y_to[1])),
            15: (lambda: (a_side.at[c, 1], a_side_in.at[c, 1], y_to[3])),
        }[kind]()
        return remote(src, dst, send.at[kind, c], recv.at[kind, c], peer)

    def here(k, c):
        src, dst = {
            0: (lambda: (cot.at[:, columns(c)], cots.at[c, 0])),
            1: (lambda: (states.at[0, :, :, columns(c)], w_in.at[lax.rem(c, 3), :, MOVE : MOVE + OLD])),
            2: (lambda: (states.at[1:3, 1, :, columns(c)], m_in.at[lax.rem(c, 2)])),
            3: (lambda: (states.at[:, 0, :, columns(c)], ext.at[lax.rem(c, 2), :, MOVE : MOVE + OLD])),
        }[k]()
        return pltpu.make_async_copy(src, dst, local.at[k, c])

    def mine(k):
        if k < 3:
            source, target = parts(y)[k]
            src, dst = tokens.at[:, source], tok.at[0, :, target]
        elif k == 3:
            src, dst = states.at[:, :, :MOVE], e_head
        else:
            src, dst = states.at[:, :, OLD - 3 * MOVE :], e_tail.at[:, :, : 3 * MOVE]
        return pltpu.make_async_copy(src, dst, misc_local.at[k])

    lost_group = failed[member]
    old_start = old_bounds[dp, member]
    old_len = old_bounds[dp, member + 1] - old_start
    new_start = new_bounds[dp, member]
    new_len = new_bounds[dp, member + 1] - new_start
    back_start = old_bounds[next_group, member]
    back_len = old_bounds[next_group, member + 1] - back_start
    mean_start = ROWS * member
    lost_use = old_len * (lost_group == dp).astype(jnp.int32)
    own_use = old_len - lost_use
    back_use = back_len * (lost_group == next_group).astype(jnp.int32)

    def window(ref, start, usable):
        shift = start - mean_start + NEAR
        place = rows_of(OLD) - shift
        return jnp.where((place >= 0) & (place < usable), rows_from(ref, MOVE - shift, OLD, (16, 8)), 0.0).astype(BF)

    def back_window(c):
        here(1, c).wait()
        w_back[c] = window(w_in.at[lax.rem(c, 3), 1], back_start, back_use)

    def windows(c):
        slot = lax.rem(c, 3)

        @pl.when(c > 0)
        def _():
            back_window(c)
            w_copy(c).start()

        w_mine[lax.rem(c, 4)] = window(w_in.at[slot, 0], old_start, own_use)

        @pl.when(c + 3 < count)
        def _():
            here(1, c + 3).start()

    def rim_rows():
        mine(3).wait()
        mine(4).wait()
        row = rows_of(MOVE)

        @pl.loop(0, count)
        def _(c):
            for number, (length, usable, rim) in enumerate(((old_len, own_use, r_mine), (back_len, back_use, r_back))):
                some = row < usable
                for state in range(3):
                    head = e_head[state, number, :, columns(c)]
                    tail = rows_from(e_tail.at[state, number, :, columns(c)], length - SHORT, MOVE, (32, 16, 8))
                    rim[0, c, state] = jnp.where(some, head, 0.0).astype(BF)
                    rim[1, c, state] = jnp.where(some, tail, 0.0).astype(BF)

    def moments(c):
        here(2, c).wait()

        @pl.when(c >= 4)
        def _():
            m_copy(c - 4).wait_send()

        m_back[lax.rem(c, 4)] = m_in[lax.rem(c, 2)].astype(BF)
        m_copy(c).start()

        @pl.when(c + 2 < count)
        def _():
            here(2, c + 2).start()

    def gather(c):
        copy(4, c).start()
        copy(5, c).start()
        w_copy(c).wait_recv()
        ws[c, 0] = w_mine[lax.rem(c, 4)] + w_arr[c]
        copy(0, c).start()
        copy(1, c).start()

    def hand_on(c):
        for kind in (0, 1, 4, 5):
            copy(kind, c).wait_recv()
            copy(kind + 2, c).start()

    def multiply(c):
        slot = lax.rem(c, RING)
        here(0, c).wait()
        copy(6, c).wait_recv()
        copy(7, c).wait_recv()

        @pl.loop(0, TALL // OLD)
        def _(i):
            rows = pl.ds(pl.multiple_of(i * OLD, 16), OLD)
            taken = pl.ds(pl.multiple_of(i * OLD + SKIP, 16), OLD)
            g_all[slot, rows] = jnp.dot(
                tok_t[taken], cots[c].reshape(SIDE * ROWS, CUT), preferred_element_type=F32
            )

        far = pl.ds(pl.multiple_of(lax.rem(z + 2, SIDE) * ROWS + NEAR, NEAR), NEW)
        g_opp[c] = g_all[slot, far].astype(BF)
        copy(8, c).start()
        copy(9, c).start()
        copy(2, c).wait_recv()
        copy(3, c).wait_recv()
        for p in range(SIDE):
            source = lax.rem(p - z + SIDE, SIDE)
            at = LANE - NEAR + ROWS * p
            piece = ws[c, source].astype(F32)
            if p == 0:
                wk_wide[at : at + MOVE] = piece[:MOVE]
            else:
                wk_wide[at : at + MOVE] = wk_wide[at : at + MOVE] + piece[:MOVE]
            wk_wide[at + MOVE : at + OLD] = piece[MOVE:]
        wk[...] = wk_wide[...].astype(BF)

        a_opp[c] = jnp.dot(tok[2], wk[...], preferred_element_type=F32).astype(BF)
        copy(12, c).start()
        copy(13, c).start()

        @pl.loop(0, 3)
        def _(k):
            a_all[slot, k] = jnp.dot(tok[k + k // 2], wk[...], preferred_element_type=F32)

    def add_on(c):
        slot = lax.rem(c, RING)
        copy(8, c).wait_recv()
        copy(9, c).wait_recv()
        up = pl.multiple_of(lax.rem(z + 1, SIDE) * ROWS + NEAR, NEAR)
        down = pl.multiple_of(lax.rem(z + 3, SIDE) * ROWS + NEAR, NEAR)
        g_side[c, 0, :G_HALF] = (g_all[slot, pl.ds(up, G_HALF)] + g_opp_in[c, :G_HALF].astype(F32)).astype(BF)
        g_side[c, 0, G_HALF:] = g_all[slot, pl.ds(up + G_HALF, NEW - G_HALF)].astype(BF)
        g_side[c, 1, :G_HALF] = g_all[slot, pl.ds(down, G_HALF)].astype(BF)
        g_side[c, 1, G_HALF:] = (
            g_all[slot, pl.ds(down + G_HALF, NEW - G_HALF)] + g_opp_in[c, G_HALF:].astype(F32)
        ).astype(BF)
        copy(10, c).start()
        copy(11, c).start()
        copy(12, c).wait_recv()
        copy(13, c).wait_recv()
        a_side[c, 0, :A_HALF] = (a_all[slot, 1, :A_HALF] + a_opp_in[c, :A_HALF].astype(F32)).astype(BF)
        a_side[c, 0, A_HALF:] = a_all[slot, 1, A_HALF:].astype(BF)
        a_side[c, 1, :A_HALF] = a_all[slot, 2, :A_HALF].astype(BF)
        a_side[c, 1, A_HALF:] = (a_all[slot, 2, A_HALF:] + a_opp_in[c, A_HALF:].astype(F32)).astype(BF)
        copy(14, c).start()
        copy(15, c).start()

    def finish(c):
        slot = lax.rem(c, RING)
        at = lax.rem(c, 2)
        row = rows_of(OLD)
        here(3, c).wait()
        m_copy(c).wait_recv()
        w_pad[:OLD] = w_arr[c].astype(F32)
        moved = []
        for state in range(3):
            if state == 0:
                back = rows_from(w_pad, old_start - mean_start + NEAR, OLD, (16, 8))
            else:
                back = m_arr[c, state - 1].astype(F32)
            r_pad[2 * MOVE : 3 * MOVE] = rims[0, c, state].astype(F32)
            late = rows_from(r_pad, 2 * MOVE - (old_len - SHORT), 3 * MOVE, (32, 16, 8))
            value = jnp.where(row < lost_use, back, ext[at, state, MOVE : MOVE + OLD])
            value = jnp.where(row < old_len, value, 0.0)
            ext[at, state, :MOVE] = rims[1, c, state].astype(F32)
            ext[at, state, MOVE : MOVE + SHORT] = value[:SHORT]
            ext[at, state, MOVE + SHORT : MOVE + OLD] = value[SHORT:] + late[: OLD - SHORT]
            ext[at, state, MOVE + OLD : MOVE + OLD + MOVE] = late[OLD - SHORT :]
            moved.append(rows_from(ext.at[at, state], MOVE + new_start - old_start, NEW, (32, 16, 8)))
        copy(14, c).wait_recv()
        copy(15, c).wait_recv()
        act[:, columns(c)] = (a_all[slot, 0] + a_side_in[c, 0].astype(F32) + a_side_in[c, 1].astype(F32)).astype(BF)
        copy(10, c).wait_recv()
        copy(11, c).wait_recv()
        rows = pl.ds(pl.multiple_of(z * ROWS + NEAR, NEAR), NEW)
        g_pad[:NEW] = g_all[slot, rows] + g_side_in[c, 0].astype(F32) + g_side_in[c, 1].astype(F32)
        grad = rows_from(g_pad, new_start - mean_start + FAR, NEW, (32, 16, 8))
        weight, one, two = moved
        one = beta_one * one + (1.0 - beta_one) * grad
        two = beta_two * two + (1.0 - beta_two) * grad * grad
        direction = one / correct_one / (jnp.sqrt(two / correct_two) + epsilon) + decay_rate * weight
        inside = rows_of(NEW) < new_len

        new_states[0, :, columns(c)] = jnp.where(inside, weight - learn_rate * direction, 0.0)
        new_states[1, :, columns(c)] = jnp.where(inside, one, 0.0)
        new_states[2, :, columns(c)] = jnp.where(inside, two, 0.0)

    for c in range(3):
        here(1, c).start()
    for k in range(5):
        mine(k).start()
    for c in range(2):
        here(2, c).start()

    @pl.loop(0, count)
    def _(c):
        here(0, c).start()

    wk_wide[:LANE] = jnp.zeros((LANE, CUT), F32)
    wk_wide[LANE + SIDE * ROWS :] = jnp.zeros((LANE, CUT), F32)
    r_pad[...] = jnp.zeros(r_pad.shape, F32)
    back_window(0)
    pl.semaphore_wait(barrier, len(peers))
    for r in (1, 3, 2):
        for k in range(3):
            tok_copy(r, k).start()
    w_copy(0).start()
    first = -PRE

    @pl.loop(0, count + END + PRE)
    def _(step):
        t = step + first

        @pl.when(t + PRE < count)
        def _():
            windows(t + PRE)

        @pl.when((t + AHEAD >= 0) & (t + AHEAD < count))
        def _():
            gather(t + AHEAD)

        @pl.when(t == -AHEAD)
        def _():
            rim_rows()
            rim_copy(0).start()

        @pl.when(t == TOK_ONE)
        def _():
            for r in (1, 3, 2):
                for k in range(3):
                    tok_copy(r, k).wait_recv()
                x_copy(SIDE - r, 0).start()
                x_copy(SIDE - r, 1).start()
                mate_copy(SIDE - r, 0).start()

        @pl.when((t + HAND >= 0) & (t + HAND < count))
        def _():
            hand_on(t + HAND)

        @pl.when((t + MOM >= 0) & (t + MOM < count))
        def _():
            moments(t + MOM)

        @pl.when(t == -1)
        def _():
            rim_copy(0).wait_recv()
            r_mine[...] = r_mine[...] + r_arr[...]
            rim_copy(1).start()
            rim_copy(2).start()

        @pl.when(t == TOK_TWO)
        def _():
            for k in range(3):
                mine(k).wait()
            tok_t[:, :ROWS] = tok[0].T
            for k in (3, 1, 2):
                x_copy(k, 0).wait_recv()
                x_copy(k, 1).wait_recv()
                mate_copy(k, 1).start()

        @pl.when(t == TOK_END)
        def _():
            for k in (3, 1, 2):
                mate_copy(k, 0).wait_recv()
                mate_copy(k, 1).wait_recv()
                tok_t[:, ROWS * k : ROWS * (k + 1)] = tok[k].T

        @pl.when((t >= 0) & (t < count))
        def _():
            multiply(t)

        @pl.when((t >= ADD) & (t < count + ADD))
        def _():
            add_on(t - ADD)

        @pl.when((t >= END - LOAD) & (t < count + END - LOAD))
        def _():
            here(3, t - END + LOAD).start()

        @pl.when(t == END)
        def _():
            rim_copy(1).wait_recv()
            rim_copy(2).wait_recv()

        @pl.when(t >= END)
        def _():
            finish(t - END)

    @pl.loop(0, count)
    def _(c):
        for kind in range(16):
            copy(kind, c).wait_send()
        w_copy(c).wait_send()

    for c in range(count - 4, count):
        m_copy(c).wait_send()
    for r in (1, 2, 3):
        for k in range(3):
            tok_copy(r, k).wait_send()
        for k in range(2):
            x_copy(r, k).wait_send()
            mate_copy(r, k).wait_send()
    for k in range(3):
        rim_copy(k).wait_send()


def body(old_states, old_bounds, new_bounds, failed, tokens, cotangent):
    width = cotangent.shape[1]
    count = width // CUT
    smem = pl.BlockSpec(memory_space=pltpu.SMEM)
    hbm = pl.BlockSpec(memory_space=pl.ANY)
    shape = jax.ShapeDtypeStruct
    vm = pltpu.VMEM
    dma = pltpu.SemaphoreType.DMA
    new_states, act = pl.pallas_call(
        lambda *refs: exchange(count, *refs),
        in_specs=[smem, smem, smem, hbm, hbm, hbm],
        out_specs=[pl.BlockSpec(memory_space=vm)] * 2,
        out_shape=[vm((3, NEW, width), F32), vm((ROWS, width), BF)],
        scratch_shapes=[
            vm((3, 2, OLD + 2 * MOVE + 8, CUT), F32),
            vm((2, 2, OLD, CUT), F32),
            vm((2, 3, NEW + SPARE, CUT), F32),
            vm((3, 2, MOVE, width), F32),
            vm((3, 2, MOVE + SPARE, width), F32),
            vm((SIDE, ROWS, DEPTH), BF),
            vm((DEPTH, SIDE * ROWS), BF),
            vm((count, SIDE, ROWS, CUT), BF),
            vm((count, SIDE, OLD, CUT), BF),
            vm((DEPTH, CUT), F32),
            vm((DEPTH, CUT), BF),
            vm((4, OLD, CUT), BF),
            vm((count, OLD, CUT), BF),
            vm((count, OLD, CUT), BF),
            vm((4, 2, OLD, CUT), BF),
            vm((count, 2, OLD, CUT), BF),
            vm((2, count, 3, MOVE, CUT), BF),
            vm((2, count, 3, MOVE, CUT), BF),
            vm((2, count, 3, MOVE, CUT), BF),
            vm((2, count, 3, MOVE, CUT), BF),
            vm((RING, TALL, CUT), F32),
            vm((RING, 3, ROWS, CUT), F32),
            vm((count, NEW, CUT), BF),
            vm((count, NEW, CUT), BF),
            vm((count, 2, NEW, CUT), BF),
            vm((count, 2, NEW, CUT), BF),
            vm((count, ROWS, CUT), BF),
            vm((count, ROWS, CUT), BF),
            vm((count, 2, ROWS, CUT), BF),
            vm((count, 2, ROWS, CUT), BF),
            vm((NEW + SPARE, CUT), F32),
            vm((OLD + SPARE, CUT), F32),
            vm((3 * MOVE + SPARE, CUT), F32),
            dma((16, count)),
            dma((16, count)),
            dma((4, count)),
            dma((SIDE, 3)),
            dma((SIDE, 3)),
            dma((SIDE, 2)),
            dma((SIDE, 2)),
            dma((SIDE, 2)),
            dma((SIDE, 2)),
            dma((2, count)),
            dma((2, count)),
            dma((3,)),
            dma((3,)),
            dma((5,)),
        ],
        compiler_params=pltpu.CompilerParams(
            collective_id=0, has_side_effects=True, vmem_limit_bytes=54 * 2**20
        ),
        name="exchange",
    )(old_bounds, new_bounds, failed, old_states, tokens, cotangent)
    return new_states, act


def solution(mesh):
    in_specs = (
        P(None, None, ("dp", "fsdp"), None),
        P(),
        P(),
        P(),
        P("fsdp", None),
        P("fsdp", "dp"),
    )
    out_specs = (P(None, ("dp", "fsdp"), None), P("fsdp", "dp"))
    return jax.shard_map(body, mesh=mesh, in_specs=in_specs, out_specs=out_specs, check_vma=False)
```
